32 devices in a mesh: leaf: 8 (over z, x), lvl: 4 (over y, core).
Axes of the slice: x: 2, y: 2, z: 4, core: 2. Of those that a mesh axis runs over, the one named last changes fastest.
Arguments:
- offsets: float32 [3, 16384], P(None, 'leaf'), may hold values from -0.5 to 0.5
- vel_cot: float32 [3, 16384], P(None, 'leaf'), may hold values from -0.18 to 0.18
- m2l_ops: bfloat16 [16, 456, 456], P('lvl'), may hold values from -0.25 to 0.25
- child_ops: bfloat16 [8, 456, 456], P('lvl'), may hold values from -0.25 to 0.25
- check_map: float32 [456, 456], replicated, may hold values from -0.015625 to 0.015625
- leaf_dest: int32 [4, 256, 4, 1], P('lvl', 'leaf'), may hold values from 0 to 7; in each aligned block of 128 rows (0 to 127, 128 to 255, ..., all dimensions but the last counted through in order) at most 32 rows name the same one
- leaf_slot: int32 [4, 256, 4], P('lvl', 'leaf'), may hold values from 0 to 31
- coarse_dest: int32 [4, 32, 4, 1], P('lvl'), may hold values from 0 to 7
- coarse_slot: int32 [4, 32, 4], P('lvl'), may hold values from 0 to 3
- near_box: int32 [256, 16], P('leaf', 'lvl'), may hold values from 0 to 31
- near_dir: int32 [256, 16], P('leaf', 'lvl'), may hold values from 0 to 26
Outputs:
- force_cot: float32 [3, 16384], P(None, 'leaf')
The draws below stay inside these ranges and needn't reach their ends.
Inputs may be any that keep to these rules, and one draw needn't show every extreme that they name: `leaf_dest`: in the rows of one device (aligned blocks of 128 rows in the order of the leading dimensions) no subtree is named more than 32 times. `near_box`: A place among the 32 leaf boxes of the same subtree.
All inputs are finite; a program needn't handle non-finite values.
Results may differ from the reference program's by a relative error of at most 0.0095.
Values may be sent and summed in bfloat16 or wider, within the bound.
No kernel may reach another device: no remote copies, remote signals or barrier semaphores. Data moves between devices by JAX's collectives and lax.ppermute only.
A program may use at most 64 MiB of HBM per device.

```python
import math
import jax
import jax.numpy as jnp
import numpy as np
from jax import lax

SIDE = 6
M = 456
CLASSES = 16
NEAR = 16
LB_DEV = 32
PPB = 64
LEAF = 256
PARENT = 32
CB_DEV = 4
PARTICLES = 16384
CL_DEV = 4
ITEMS = 128
CAP = 32
N_LEAF = 8
N_LVL = 4


def with_ends(entries, rng, least, high):
    shape = entries.shape
    spot = [jax.random.randint(jax.random.fold_in(rng, axis), (), 0, shape[axis]) for axis in range(len(shape))]
    entries = entries.at[tuple(spot)].set(least)
    longest = shape.index(max(shape))
    spot[longest] = (spot[longest] + 1) % shape[longest]
    return entries.at[tuple(spot)].set(high)


def level_of(own_key, extent, pieces, smallest, high):
    gain, own = 1.0, jax.random.fold_in(own_key, 6)
    for position, shards_of in pieces:
        heights = jnp.exp(jax.random.uniform(jax.random.fold_in(own, position), (shards_of,), jnp.float32, smallest / len(pieces), high / len(pieces)))
        gain = gain * jnp.repeat(heights, extent[position] // shards_of).reshape([-1 if axis == position else 1 for axis in range(len(extent))])
    return gain


def assign_block(key, own, number, rows, count, top, bound, skew):
    sequence = jax.random.permutation(key, count)
    crowded, ordinary = shares(count, rows * top, bound, skew, True), shares(count, rows * top, bound, skew, False)
    places = jnp.arange(count)

    def named(tallies, offset_by):
        used = int((tallies > 0).sum())
        fixed = max(1, used // 4)
        moved = fixed + (places - fixed + offset_by * (used - fixed)) % max(1, count - fixed)
        return jnp.zeros((count,), jnp.int32).at[sequence[jnp.where(places < fixed, places, moved)]].set(jnp.asarray(tallies, jnp.int32))

    tallies = jnp.where(number % 4 == 0, named(crowded, number // 4), named(ordinary, number - number // 4 - 1))
    mixed = jax.random.permutation(jax.random.fold_in(own, 3), count)
    donor, taker = mixed[0:count // 2 * 2:2], mixed[1:count // 2 * 2:2]
    room = jnp.minimum(tallies[donor] - 1, bound - tallies[taker]) // 2
    room = jnp.where((donor == sequence[0]) | (taker == sequence[0]) | (tallies[taker] == 0), 0, jnp.maximum(room, 0))
    moved = jax.random.randint(jax.random.fold_in(own, 4), (count // 2,), 0, 1 << 20) % (room + 1)
    tallies = tallies.at[donor].add(-moved).at[taker].add(moved)
    members = jnp.searchsorted(jnp.cumsum(tallies), jnp.arange(rows * top), side="right").astype(jnp.int32)
    table = members.reshape(top, rows).T
    table = table[jax.random.permutation(jax.random.fold_in(own, 1), rows)]
    offset_by = jax.random.randint(jax.random.fold_in(own, 2), (rows, 1), 0, top)
    return jnp.take_along_axis(table, (jnp.arange(top)[None, :] + offset_by) % top, axis=1)


def shares(number_of, total, bound, lean, full):
    weights = [(1 << 20) // math.isqrt(standing ** lean) + 1 for standing in range(1, number_of + 1)]
    largest = bound if full else min(bound, max(-(-total // number_of), total * weights[0] // sum(weights)))
    least = 1 if total - largest >= number_of - 1 else 0
    holding, surplus = [largest] + [least] * (number_of - 1), total - largest - least * (number_of - 1)
    while surplus > 0:
        movable = [i for i in range(1, number_of) if holding[i] < largest] or [i for i in range(1, number_of) if holding[i] < bound]
        whole, remaining = sum([weights[i] for i in movable]), surplus
        for i in movable:
            more = min(bound - holding[i], max(1, remaining * weights[i] // whole), surplus)
            holding[i] = holding[i] + more
            surplus = surplus - more
    return np.array(holding)


def centred(rng, shape, deviation, bound, cuts=(), held_as=jnp.bfloat16):
    drawn = jax.random.normal(rng, shape, jnp.float32) * deviation
    if len(cuts) > 0:
        drawn = level_of(rng, shape, cuts, -0.22, 0.18) * drawn
    return jnp.clip(drawn, min=-bound, max=bound).astype(held_as)


def setup_inputs(seed: int = 0) -> dict:
    key_list = jax.random.split(jax.random.key(seed), 12)
    offsets = jnp.clip(jax.random.uniform(key_list[0], (3, PARTICLES), jnp.float32, -0.5, 0.5) * level_of(key_list[0], (3, PARTICLES), ((1, 8),), -0.4, 0.0), -0.5, 0.5)
    vel_cot = centred(key_list[1], (3, PARTICLES), 0.03, 0.18, ((1, 8),), jnp.float32)
    m2l_ops = centred(key_list[2], (CLASSES, M, M), M ** -0.5, 0.25, ((0, 4),))
    child_ops = centred(key_list[3], (8, M, M), M ** -0.5, 0.25, ((0, 4),))
    check_map = centred(key_list[4], (M, M), (M * 256) ** -0.5, 0.015625, (), jnp.float32)
    leaf_dest_keys = jax.random.split(jax.random.fold_in(key_list[5], 1), N_LVL * LEAF * CL_DEV // ITEMS)
    leaf_dest_turns = jax.random.permutation(jax.random.fold_in(key_list[5], 3), N_LVL * LEAF * CL_DEV // ITEMS)
    leaf_dest = jax.vmap(lambda own, number: assign_block(jax.random.fold_in(key_list[5], 2), own, number, ITEMS, N_LEAF, 1, CAP, 2))(leaf_dest_keys, leaf_dest_turns).reshape((N_LVL, LEAF, CL_DEV, 1))
    leaf_slot = with_ends(jax.random.randint(key_list[6], (N_LVL, LEAF, CL_DEV), 0, LB_DEV), jax.random.fold_in(key_list[6], 1), 0, LB_DEV - 1).astype(jnp.int32)
    coarse_dest = with_ends(jax.random.randint(key_list[7], (N_LVL, PARENT, CL_DEV, 1), 0, N_LEAF), jax.random.fold_in(key_list[7], 1), 0, N_LEAF - 1).astype(jnp.int32)
    coarse_slot = with_ends(jax.random.randint(key_list[8], (N_LVL, PARENT, CL_DEV), 0, CB_DEV), jax.random.fold_in(key_list[8], 1), 0, CB_DEV - 1).astype(jnp.int32)
    near_box = with_ends(jax.random.randint(key_list[9], (LEAF, NEAR), 0, LB_DEV), jax.random.fold_in(key_list[9], 1), 0, LB_DEV - 1).astype(jnp.int32)
    near_dir = with_ends(jax.random.randint(key_list[10], (LEAF, NEAR), 0, 27), jax.random.fold_in(key_list[10], 1), 0, 26).astype(jnp.int32)
    return {"offsets": offsets, "vel_cot": vel_cot, "m2l_ops": m2l_ops, "child_ops": child_ops, "check_map": check_map, "leaf_dest": leaf_dest, "leaf_slot": leaf_slot, "coarse_dest": coarse_dest, "coarse_slot": coarse_slot, "near_box": near_box, "near_dir": near_dir}


EPSILON2 = 0.01
RADIUS = 0.525


def surface_points(edge_count):
    levels = np.linspace(-1.0, 1.0, edge_count)
    lattice = np.stack(np.meshgrid(levels, levels, levels, indexing="ij"), 0).reshape(3, -1)
    on_shell = np.max(np.abs(lattice), 0) > 1.0 - 1e-9
    return jnp.asarray(lattice[:, on_shell] * RADIUS, jnp.float32)


def stokes_apply(relative, source):
    squared = jnp.sum(relative * relative, axis=0)
    weights = (squared + EPSILON2) ** -1.5
    spread = source[..., None, :]
    along = jnp.sum(relative * spread, axis=0)
    return jnp.sum(weights * ((squared + 2.0 * EPSILON2) * spread + relative * along), axis=-1)


def to_surface(points, vectors, shell):
    relative = shell[:, None, :, None] - points[:, :, None, :]
    values = stokes_apply(relative, vectors)
    return values.transpose(1, 0, 2).reshape(values.shape[1], -1)


def from_surface(points, density, shell):
    source = density.reshape(density.shape[0], 3, -1).transpose(1, 0, 2)
    relative = points[:, :, :, None] - shell[:, None, None, :]
    return stokes_apply(relative, source)


def directions(codes):
    return jnp.stack([codes // 9 - 1, codes // 3 % 3 - 1, codes % 3 - 1], 0).astype(jnp.float32)


def near_terms(points, src_points, src_vectors, shifts):
    moved = src_points + shifts[..., None]
    relative = points[:, :, None, :, None] - moved[:, :, :, None, :]
    return jnp.sum(stokes_apply(relative, src_vectors), axis=2)


def reference(offsets, vel_cot, m2l_ops, child_ops, check_map, leaf_dest, leaf_slot, coarse_dest, coarse_slot, near_box, near_dir):
    shell = surface_points(SIDE)
    points = offsets.reshape(3, LEAF, PPB)
    vectors = vel_cot.reshape(3, LEAF, PPB)
    blocks = LEAF // 8
    point_blocks = points.reshape(3, blocks, 8, PPB).transpose(1, 0, 2, 3)
    vector_blocks = vectors.reshape(3, blocks, 8, PPB).transpose(1, 0, 2, 3)
    local_float = lax.map(lambda packed: to_surface(packed[0], packed[1], shell), (point_blocks, vector_blocks))
    leaf_local = local_float.reshape(LEAF, M).astype(jnp.bfloat16)

    owners = leaf_dest[..., 0].transpose(0, 2, 1).reshape(CLASSES, LEAF)
    places = leaf_slot.transpose(0, 2, 1).reshape(CLASSES, LEAF)
    sources = (owners * LB_DEV + places).astype(jnp.int32)

    def leaf_class(total, packed):
        operator, targets = packed
        term = jnp.dot(leaf_local, operator, preferred_element_type=jnp.float32).astype(jnp.bfloat16)
        return total + jax.ops.segment_sum(term.astype(jnp.float32), targets, num_segments=LEAF), None

    leaf_mult, _ = lax.scan(leaf_class, jnp.zeros((LEAF, M), jnp.float32), (m2l_ops, sources))

    children = leaf_local.reshape(PARENT, 8, M)
    parent_float = jnp.zeros((PARENT, M), jnp.float32)
    for octant in range(8):
        parent_float = parent_float + jnp.dot(children[:, octant], child_ops[octant], preferred_element_type=jnp.float32)
    parent_local = parent_float.astype(jnp.bfloat16)

    coarse_global = coarse_dest[..., 0] * CB_DEV + coarse_slot
    coarse_ids = coarse_global.transpose(0, 2, 1).reshape(CLASSES, PARENT).astype(jnp.int32)

    def coarse_class(total, packed):
        operator, targets = packed
        term = 0.5 * jnp.dot(parent_local, operator, preferred_element_type=jnp.float32)
        return total + jax.ops.segment_sum(term, targets, num_segments=PARENT), None

    parent_float, _ = lax.scan(coarse_class, jnp.zeros((PARENT, M), jnp.float32), (m2l_ops, coarse_ids))
    parent_mult = parent_float.astype(jnp.bfloat16)
    lowered = jnp.stack([jnp.dot(parent_mult, child_ops[octant].T, preferred_element_type=jnp.float32) for octant in range(8)], 1)
    total_mult = leaf_mult + lowered.reshape(LEAF, M)
    check_cot = jnp.dot(total_mult, check_map, precision=lax.Precision.HIGHEST)

    check_blocks = check_cot.reshape(blocks, 8, M)
    far_blocks = lax.map(lambda packed: from_surface(packed[0], packed[1], shell), (point_blocks, check_blocks))
    far_cot = far_blocks.transpose(1, 0, 2, 3).reshape(3, PARTICLES)

    bases = (jnp.arange(LEAF, dtype=jnp.int32) // LB_DEV) * LB_DEV
    neighbours = (bases[:, None] + near_box).astype(jnp.int32)
    shifts = directions(near_dir)
    neighbour_blocks = neighbours.reshape(blocks, 8, NEAR)
    shift_blocks = shifts.reshape(3, blocks, 8, NEAR).transpose(1, 0, 2, 3)

    def near_block(packed):
        here, chosen, moved = packed
        return near_terms(here, points[:, chosen], vectors[:, chosen], moved)

    near_blocks = lax.map(near_block, (point_blocks, neighbour_blocks, shift_blocks))
    near_cot = near_blocks.transpose(1, 0, 2, 3).reshape(3, PARTICLES)
    return far_cot + near_cot
```

```python
import jax
import jax.numpy as jnp
import numpy as np
from jax import lax
from jax.experimental import pallas as pl
from jax.experimental.pallas import tpu as pltpu
from jax.sharding import PartitionSpec as P

SIDE = 6
EPSILON2 = 0.01
RADIUS = 0.525
LANES = 128
F32 = jnp.float32
BF16 = jnp.bfloat16
VMEM = pl.BlockSpec(memory_space=pltpu.VMEM)
SMEM = pl.BlockSpec(memory_space=pltpu.SMEM)
NN = (((1,), (0,)), ((), ()))
NT = (((1,), (1,)), ((), ()))
TN = (((0,), (0,)), ((), ()))


def surface_points(edge_count):
    levels = np.linspace(-1.0, 1.0, edge_count)
    lattice = np.stack(np.meshgrid(levels, levels, levels, indexing="ij"), 0).reshape(3, -1)
    on_shell = np.max(np.abs(lattice), 0) > 1.0 - 1e-09
    return np.asarray(lattice[:, on_shell] * RADIUS, np.float32)


def dot(a, b, dims=NN):
    return lax.dot_general(a, b, dims, preferred_element_type=F32)


def iota(shape, axis):
    return lax.broadcasted_iota(jnp.int32, shape, axis)


def stokeslet(d, v):
    r2 = d[0] * d[0] + d[1] * d[1] + (d[2] * d[2] + EPSILON2)
    rs = lax.rsqrt(r2)
    weight = rs * (rs * rs)
    scale = rs + EPSILON2 * weight
    along = weight * (d[0] * v[0] + d[1] * v[1] + d[2] * v[2])
    return [scale * v[c] + along * d[c] for c in range(3)]


def call(body, outs, cost, scratch=(), ins=None, vmem=24):
    return pl.pallas_call(
        body,
        out_shape=outs,
        in_specs=ins,
        out_specs=jax.tree.map(lambda _: VMEM, outs),
        scratch_shapes=list(scratch),
        cost_estimate=pl.CostEstimate(flops=cost, bytes_accessed=1 << 20, transcendentals=0),
        compiler_params=pltpu.CompilerParams(vmem_limit_bytes=vmem << 20),
    )


def shape(dims, dtype):
    return jax.ShapeDtypeStruct(tuple(dims), dtype)


def surface_block(points, vectors, shell_ref, fields, column):
    count = shell_ref.shape[0]
    for row in range(0, count, 8):
        d = [shell_ref[row : row + 8, c : c + 1] - points[c] for c in range(3)]
        for c, value in enumerate(stokeslet(d, vectors)):
            fields[c * count + row : c * count + row + 8, column] = value


def blocks128(matrix):
    width = matrix.shape[1]
    fill = -width % LANES
    if fill:
        matrix = jnp.concatenate([matrix, jnp.zeros((matrix.shape[0], fill), matrix.dtype)], 1)
    return [matrix[:, k : k + LANES] for k in range(0, width, LANES)]


def local(
    offsets,
    vel_cot,
    m2l_ops,
    child_ops,
    check_map,
    leaf_dest,
    leaf_slot,
    coarse_dest,
    coarse_slot,
    near_box,
    near_dir,
):
    shell_np = surface_points(SIDE)
    count = shell_np.shape[1]
    width = m2l_ops.shape[1]
    classes = m2l_ops.shape[0]
    octants = child_ops.shape[0]
    boxes, slots = near_box.shape
    per_box = offsets.shape[1] // boxes
    parents = boxes // 8
    own = parents * octants
    leaves = lax.axis_size("leaf")
    lvls = lax.axis_size("lvl")
    pieces = -(-width // LANES)
    group = octants * per_box
    groups = parents * lvls
    assert group == LANES and own == 8 and parents == 4 and lvls * octants == 8
    up_rows = pieces * parents
    leaf_rows = pieces * boxes
    own_rows = pieces * own
    tall = groups * LANES
    shell = jnp.asarray(np.pad(shell_np.T, ((0, 0), (0, LANES - 3))))

    leaf_owner = leaf_dest.transpose(0, 2, 3, 1)[0]
    leaf_place = leaf_slot.transpose(0, 2, 1)[0]
    coarse_owner = coarse_dest.transpose(0, 2, 3, 1)[0]
    coarse_place = coarse_slot.transpose(0, 2, 1)[0]
    near_q = near_box.T
    near_d = near_dir.T

    def lanes_of(parent, lvl):
        return pl.ds(pl.multiple_of((parent * lvls + lvl) * LANES, LANES), LANES)

    def rows3(ref, lanes):
        return [ref[c : c + 1, lanes] for c in range(3)]

    def up_body(offsets_ref, vel_ref, child_ref, shell_ref, up_ref, fields):
        me = lax.axis_index("lvl")
        for p in range(parents):
            lanes = lanes_of(p, me)
            surface_block(
                rows3(offsets_ref, lanes),
                rows3(vel_ref, lanes),
                shell_ref,
                fields,
                slice(p * LANES, (p + 1) * LANES),
            )
        here = parents * LANES
        lane = iota((8 * octants, here), 1)
        row = iota((8 * octants, here), 0)
        target = (lane % LANES) // per_box * 8 + lane // LANES
        pick = (row == target).astype(F32).astype(BF16)
        leaf = dot(pick, fields[...].astype(BF16), NT).astype(BF16)
        total = dot(leaf[0:8], child_ref[0])
        for o in range(1, octants):
            total = total + dot(leaf[8 * o : 8 * o + 8], child_ref[o])
        for k, block in enumerate(blocks128(total)):
            up_ref[k * parents : (k + 1) * parents, :] = block[0:parents]

    up = call(
        up_body,
        shape((up_rows, LANES), F32),
        20_000_000,
        [pltpu.VMEM((3 * count, parents * LANES), F32)],
        [VMEM] * 4,
    )(offsets, vel_cot, child_ops, shell)

    def shifted(value, k):
        return lax.ppermute(value, "lvl", [(i, (i + k) % lvls) for i in range(lvls)])

    ups = [up] + [shifted(up, k) for k in range(1, lvls)]

    def push_body(offsets_ref, vel_ref, m2l_ref, shell_ref, owner_ref, place_ref, out_ref, fields):
        def block(j, _):
            lanes = pl.ds(pl.multiple_of(j * LANES, LANES), LANES)
            surface_block(
                rows3(offsets_ref, lanes), rows3(vel_ref, lanes), shell_ref, fields, lanes
            )
            return 0

        lax.fori_loop(0, groups, block, 0)
        pick = (iota((boxes, tall), 0) == iota((boxes, tall), 1) // per_box).astype(F32)
        leaf = dot(pick.astype(BF16), fields[...].astype(BF16), NT).astype(BF16)
        total = None
        for c in range(classes):
            term = dot(leaf, m2l_ref[c]).astype(BF16)
            place = place_ref[c : c + 1, :]
            octant = lax.rem(place, 8)
            slot = (
                lax.div(octant, octants) * own
                + lax.rem(octant, octants) * parents
                + lax.div(place, 8)
            )
            code = owner_ref[c] * boxes + slot
            hit = (iota((leaves * boxes, boxes), 0) == code).astype(F32).astype(BF16)
            part = dot(hit, term)
            total = part if total is None else total + part
        for k, block_k in enumerate(blocks128(total.astype(BF16))):
            out_ref[:, k * boxes : (k + 1) * boxes, :] = block_k.reshape(leaves, boxes, LANES)

    pushed = call(
        push_body,
        shape((leaves, leaf_rows, LANES), BF16),
        80_000_000,
        [pltpu.VMEM((3 * count, tall), F32)],
        [VMEM] * 6,
        40,
    )(offsets, vel_cot, m2l_ops, shell, leaf_owner, leaf_place)

    def pack_body(pushed_ref, *refs):
        *up_refs, out_ref = refs
        total = up_refs[0][...]
        for ref in up_refs[1:]:
            total = total + ref[...]
        out_ref[:, :leaf_rows, :] = pushed_ref[...]
        out_ref[:, leaf_rows:, :] = jnp.broadcast_to(
            total.astype(BF16)[None], (leaves, up_rows, LANES)
        )

    sent = call(
        pack_body, shape((leaves, leaf_rows + up_rows, LANES), BF16), 1_000_000, (), [VMEM] * (1 + lvls)
    )(pushed, *ups)
    got = lax.all_to_all(sent, "leaf", split_axis=0, concat_axis=0, tiled=True)

    def near_body(
        q_ref, dir_ref, offsets_ref, vel_ref, owner_ref, place_ref, map_ref, near_ref, sel_ref, split_ref, source
    ):
        mapped = map_ref[...]
        high = mapped.astype(BF16)
        split_ref[0] = high
        split_ref[1] = (mapped - high.astype(F32)).astype(BF16)
        mine = lax.axis_index("leaf") * parents
        coarse = leaves * parents
        pick = jnp.concatenate(
            [
                (
                    owner_ref[c] * parents + place_ref[c : c + 1, :]
                    == mine + iota((8, coarse), 0) % parents
                ).astype(F32)
                for c in range(classes)
            ],
            0,
        ).astype(BF16)
        spread = (coarse, leaves * up_rows)
        lane = iota(spread, 1)
        for k in range(pieces):
            expand = (iota(spread, 0) == lane // up_rows * parents + lane % parents) & (
                lane % up_rows // parents == k
            )
            sel_ref[k] = dot(pick, expand.astype(F32).astype(BF16)).astype(BF16)

        source[...] = jnp.concatenate(
            [offsets_ref[...], vel_ref[...], jnp.zeros((2, tall), F32)], 0
        ).T
        near_ref[...] = jnp.zeros_like(near_ref)
        left = iota((8, LANES), 1) < per_box

        def block(j, _):
            lanes = pl.ds(pl.multiple_of(j * LANES, LANES), LANES)
            target = rows3(offsets_ref, lanes)
            force = [jnp.zeros((8, LANES), F32) for _ in range(3)]
            for n in range(slots):
                qs = [q_ref[n, 2 * j + h] * per_box for h in range(2)]
                codes = [dir_ref[n, 2 * j + h] for h in range(2)]
                moves = [
                    (lax.div(code, 9) - 1, lax.rem(lax.div(code, 3), 3) - 1, lax.rem(code, 3) - 1)
                    for code in codes
                ]
                here = [
                    target[c]
                    - jnp.where(left, moves[0][c].astype(F32), moves[1][c].astype(F32))
                    for c in range(3)
                ]
                for row in range(0, per_box, 8):
                    tiles = [source[pl.ds(pl.multiple_of(q + row, 8), 8), :] for q in qs]
                    both = [
                        jnp.where(left, tiles[0][:, c : c + 1], tiles[1][:, c : c + 1])
                        for c in range(6)
                    ]
                    part = stokeslet([here[c] - both[c] for c in range(3)], both[3:])
                    force = [force[c] + part[c] for c in range(3)]
            p, lvl = lax.div(j, lvls), lax.rem(j, lvls)
            for c in range(3):
                near_ref[lvl, pl.ds(p * 4 + c, 1), :] = jnp.sum(force[c], 0, keepdims=True)
            return 0

        lax.fori_loop(0, groups, block, 0)

    near, select, map_split = call(
        near_body,
        (
            shape((lvls, parents * 4, LANES), F32),
            shape((pieces, 8 * classes, leaves * up_rows), BF16),
            shape((2, width, width), BF16),
        ),
        100_000_000,
        [pltpu.VMEM((tall, 8), F32)],
        [SMEM, SMEM] + [VMEM] * 5,
        40,
    )(near_q, near_d, offsets, vel_cot, coarse_owner, coarse_place, check_map)

    def mid_body(got_ref, sel_ref, m2l_ref, near_ref, *refs):
        *out_refs, leaf_sum = refs
        me = lax.axis_index("lvl")
        leaf_sum[...] = jnp.sum(got_ref[:, :leaf_rows, :].astype(F32), 0)
        tops = got_ref[:, leaf_rows:, :].reshape(leaves * up_rows, LANES)
        chosen = jnp.concatenate([dot(sel_ref[k], tops) for k in range(pieces)], 1)
        high = chosen.astype(BF16).astype(F32)
        parts = jnp.where(iota(chosen.shape, 0) % 8 < parents, high, chosen - high)
        parts = parts[:, :width].astype(BF16)
        total = dot(parts[0:8], m2l_ref[0])
        for c in range(1, classes):
            total = total + dot(parts[8 * c : 8 * c + 8], m2l_ref[c])
        total = 0.5 * (total[0:parents] + total[parents : 2 * parents])
        total_blocks = blocks128(total)
        for k, out_ref in enumerate(out_refs):
            peer = lax.rem(me + k, lvls)
            for i, block in enumerate(total_blocks):
                out_ref[i * parents : (i + 1) * parents, :] = block.astype(out_ref.dtype)
            for i in range(pieces):
                rows = leaf_sum[pl.ds(pl.multiple_of(i * boxes + peer * own, own), own), :]
                out_ref[up_rows + i * own : up_rows + (i + 1) * own, :] = rows.astype(out_ref.dtype)
            out_ref[up_rows + own_rows :, :] = near_ref[peer].astype(out_ref.dtype)

    pay_rows = up_rows + own_rows + parents * 4
    mids = call(
        mid_body,
        tuple(shape((pay_rows, LANES), BF16 if k else F32) for k in range(lvls)),
        20_000_000,
        [pltpu.VMEM((leaf_rows, LANES), F32)],
        [VMEM] * 4,
    )(got, select, m2l_ops, near)
    mids = [mids[0]] + [shifted(mids[k], k) for k in range(1, lvls)]

    def down_body(child_ref, split_ref, offsets_ref, shell_ref, *refs):
        *mid_refs, out_ref, dens = refs
        me = lax.axis_index("lvl")
        total = mid_refs[0][...]
        for ref in mid_refs[1:]:
            total = total + ref[...].astype(F32)
        top = jnp.concatenate(
            [total[k * parents : (k + 1) * parents] for k in range(pieces)], 1
        )[:, :width].astype(BF16)
        lowered = jnp.concatenate([dot(top, child_ref[o], NT) for o in range(octants)], 0)
        leaf = jnp.concatenate(
            [total[up_rows + k * own : up_rows + (k + 1) * own] for k in range(pieces)], 1
        )[:, :width]
        mult = leaf + lowered
        high = mult.astype(BF16)
        pair = jnp.concatenate([high.astype(F32), mult - high.astype(F32)], 0).astype(BF16)
        first, second = dot(pair, split_ref[0]), dot(pair, split_ref[1])
        check = first[0:own] + first[own:] + second[0:own] + second[own:]
        high = check.astype(BF16).astype(F32)
        pair = jnp.concatenate([high, check - high], 0).astype(BF16)
        here = parents * LANES
        lane = iota((2 * own, here), 1)
        box = lane % LANES // per_box * parents + lane // LANES
        hit = (iota((2 * own, here), 0) % own == box).astype(F32).astype(BF16)
        dens[...] = dot(pair, hit, TN)
        out_ref[...] = total[up_rows + own_rows :]
        for p in range(parents):
            target = rows3(offsets_ref, lanes_of(p, me))
            lanes = slice(p * LANES, (p + 1) * LANES)
            force = [jnp.zeros((8, LANES), F32) for _ in range(3)]
            for row in range(0, count, 8):
                d = [target[c] - shell_ref[row : row + 8, c : c + 1] for c in range(3)]
                q = [dens[c * count + row : c * count + row + 8, lanes] for c in range(3)]
                part = stokeslet(d, q)
                force = [force[c] + part[c] for c in range(3)]
            for c in range(3):
                row = p * 4 + c
                out_ref[row : row + 1, :] += jnp.sum(force[c], 0, keepdims=True)

    forces = call(
        down_body,
        shape((parents * 4, LANES), F32),
        20_000_000,
        [pltpu.VMEM((3 * count, parents * LANES), F32)],
        [VMEM] * (4 + lvls),
    )(child_ops, map_split, offsets, shell, *mids)
    forces = [forces] + [shifted(forces, k) for k in range(1, lvls)]

    def join_body(*refs):
        *parts, out_ref = refs
        me = lax.axis_index("lvl")
        for k, ref in enumerate(parts):
            peer = lax.rem(me + lvls - k, lvls)
            for p in range(parents):
                out_ref[:, lanes_of(p, peer)] = ref[p * 4 : p * 4 + 3, :]

    return call(join_body, shape((3, tall), F32), 100_000, (), [VMEM] * lvls)(*forces)


def solution(mesh):
    placed = (
        P(None, "leaf"),
        P(None, "leaf"),
        P("lvl", None, None),
        P("lvl", None, None),
        P(),
        P("lvl", "leaf", None, None),
        P("lvl", "leaf", None),
        P("lvl", None, None, None),
        P("lvl", None, None),
        P("leaf", "lvl"),
        P("leaf", "lvl"),
    )
    return jax.shard_map(
        local, mesh=mesh, in_specs=placed, out_specs=P(None, "leaf"), check_vma=False
    )
```

```python
import jax
import jax.numpy as jnp
import numpy as np
from jax import lax
from jax.experimental import pallas as pl
from jax.experimental.pallas import tpu as pltpu
from jax.sharding import PartitionSpec as P

SIDE = 6
EPSILON2 = 0.01
RADIUS = 0.525
LANES = 128
F32 = jnp.float32
BF16 = jnp.bfloat16
VMEM = pl.BlockSpec(memory_space=pltpu.VMEM)
HBM = pl.BlockSpec(memory_space=pltpu.HBM)
SMEM = pl.BlockSpec(memory_space=pltpu.SMEM)
NN = (((1,), (0,)), ((), ()))
NT = (((1,), (1,)), ((), ()))
TN = (((0,), (0,)), ((), ()))


def surface_points(edge_count):
    levels = np.linspace(-1.0, 1.0, edge_count)
    lattice = np.stack(np.meshgrid(levels, levels, levels, indexing="ij"), 0).reshape(3, -1)
    on_shell = np.max(np.abs(lattice), 0) > 1.0 - 1e-09
    return np.asarray(lattice[:, on_shell] * RADIUS, np.float32)


def dot(a, b, dims=NN):
    return lax.dot_general(a, b, dims, preferred_element_type=F32)


def iota(shape, axis):
    return lax.broadcasted_iota(jnp.int32, shape, axis)


def stokeslet(d, v):
    r2 = d[0] * d[0] + d[1] * d[1] + (d[2] * d[2] + EPSILON2)
    rs = lax.rsqrt(r2)
    weight = rs * (rs * rs)
    scale = rs + EPSILON2 * weight
    along = weight * (d[0] * v[0] + d[1] * v[1] + d[2] * v[2])
    return [scale * v[c] + along * d[c] for c in range(3)]


def call(body, outs, cost, scratch=(), ins=None, vmem=24, touched=1 << 20):
    return pl.pallas_call(
        body,
        out_shape=outs,
        in_specs=ins,
        out_specs=jax.tree.map(lambda _: VMEM, outs),
        scratch_shapes=list(scratch),
        cost_estimate=pl.CostEstimate(flops=cost, bytes_accessed=touched, transcendentals=0),
        compiler_params=pltpu.CompilerParams(vmem_limit_bytes=vmem << 20),
    )


def in_hbm(*arrays):
    return [pltpu.with_memory_space_constraint(array, pltpu.HBM) for array in arrays]


def shape(dims, dtype):
    return jax.ShapeDtypeStruct(tuple(dims), dtype)


def surface_block(points, vectors, shell_ref, fields, column):
    count = shell_ref.shape[0] // 3
    for row in range(0, count, 8):
        spots = [slice(c * count + row, c * count + row + 8) for c in range(3)]
        d = [shell_ref[spots[c], :] - points[c] for c in range(3)]
        for c, value in enumerate(stokeslet(d, vectors)):
            fields[spots[c], column] = value


def blocks128(matrix):
    width = matrix.shape[1]
    fill = -width % LANES
    if fill:
        matrix = jnp.concatenate([matrix, jnp.zeros((matrix.shape[0], fill), matrix.dtype)], 1)
    return [matrix[:, k : k + LANES] for k in range(0, width, LANES)]


def local(
    offsets,
    vel_cot,
    m2l_ops,
    child_ops,
    check_map,
    leaf_dest,
    leaf_slot,
    coarse_dest,
    coarse_slot,
    near_box,
    near_dir,
):
    shell_np = surface_points(SIDE)
    count = shell_np.shape[1]
    width = m2l_ops.shape[1]
    classes = m2l_ops.shape[0]
    octants = child_ops.shape[0]
    boxes, slots = near_box.shape
    per_box = offsets.shape[1] // boxes
    parents = boxes // 8
    own = parents * octants
    leaves = lax.axis_size("leaf")
    lvls = lax.axis_size("lvl")
    pieces = -(-width // LANES)
    group = octants * per_box
    groups = parents * lvls
    assert group == LANES and own == 8 and parents == 4 and lvls * octants == 8
    up_rows = pieces * parents
    leaf_rows = pieces * boxes
    own_rows = pieces * own
    tall = groups * LANES
    shell = jnp.asarray(np.repeat(shell_np.reshape(-1, 1), LANES, 1))

    leaf_owner = leaf_dest.transpose(0, 2, 3, 1)[0]
    leaf_place = leaf_slot.transpose(0, 2, 1)[0]
    coarse_owner = coarse_dest.transpose(0, 2, 3, 1)[0]
    coarse_place = coarse_slot.transpose(0, 2, 1)[0]
    near_q = near_box.T
    near_d = near_dir.T

    def lanes_of(parent, lvl):
        return pl.ds(pl.multiple_of((parent * lvls + lvl) * LANES, LANES), LANES)

    def rows3(ref, lanes):
        return [ref[c : c + 1, lanes] for c in range(3)]

    def up_body(
        offsets_hbm, vel_hbm, child_hbm, shell_hbm, up_ref, offsets_ref, vel_ref, shell_ref, child_ref, fields, sems
    ):
        me = lax.axis_index("lvl")
        copies = [
            pltpu.make_async_copy(source, target, sems.at[i])
            for i, (source, target) in enumerate(
                (
                    (offsets_hbm, offsets_ref),
                    (vel_hbm, vel_ref),
                    (shell_hbm, shell_ref),
                    (child_hbm, child_ref),
                )
            )
        ]
        for copy in copies:
            copy.start()
        for copy in copies[:3]:
            copy.wait()
        for p in range(parents):
            lanes = lanes_of(p, me)
            surface_block(
                rows3(offsets_ref, lanes),
                rows3(vel_ref, lanes),
                shell_ref,
                fields,
                slice(p * LANES, (p + 1) * LANES),
            )
        here = parents * LANES
        lane = iota((8 * octants, here), 1)
        row = iota((8 * octants, here), 0)
        target = (lane % LANES) // per_box * 8 + lane // LANES
        pick = (row == target).astype(F32).astype(BF16)
        leaf = dot(pick, fields[...].astype(BF16), NT).astype(BF16)
        copies[3].wait()
        total = dot(leaf[0:8], child_ref[0])
        for o in range(1, octants):
            total = total + dot(leaf[8 * o : 8 * o + 8], child_ref[o])
        for k, block in enumerate(blocks128(total)):
            up_ref[k * parents : (k + 1) * parents, :] = block[0:parents]

    up, offsets, vel_cot, shell = call(
        up_body,
        (
            shape((up_rows, LANES), F32),
            shape(offsets.shape, F32),
            shape(vel_cot.shape, F32),
            shape(shell.shape, F32),
        ),
        20_000_000,
        [
            pltpu.VMEM(child_ops.shape, BF16),
            pltpu.VMEM((3 * count, parents * LANES), F32),
            pltpu.SemaphoreType.DMA((4,)),
        ],
        [HBM] * 4,
        40,
        0,
    )(*in_hbm(offsets, vel_cot, child_ops, shell))

    def shifted(value, k):
        return lax.ppermute(value, "lvl", [(i, (i + k) % lvls) for i in range(lvls)])

    ups = [up] + [shifted(up, k) for k in range(1, lvls)]

    def push_body(
        offsets_ref, vel_ref, shell_ref, m2l_hbm, owner_hbm, place_hbm, out_ref, m2l_ref, owner_ref, place_ref, fields, sems
    ):
        copies = [
            pltpu.make_async_copy(source, target, sems.at[i])
            for i, (source, target) in enumerate(
                ((m2l_hbm, m2l_ref), (owner_hbm, owner_ref), (place_hbm, place_ref))
            )
        ]
        for copy in copies:
            copy.start()
        leaf = jnp.zeros((boxes, 3 * count), F32)
        for j in range(groups):
            lanes = slice(j * LANES, (j + 1) * LANES)
            surface_block(
                rows3(offsets_ref, lanes), rows3(vel_ref, lanes), shell_ref, fields.at[j % 2], slice(None)
            )
            box = iota((boxes, LANES), 1) // per_box + j * LANES // per_box
            pick = (iota((boxes, LANES), 0) == box).astype(F32).astype(BF16)
            leaf = leaf + dot(pick, fields[j % 2].astype(BF16), NT)
        leaf = leaf.astype(BF16)
        for copy in copies:
            copy.wait()
        total = None
        for c in range(classes):
            term = dot(leaf, m2l_ref[c]).astype(BF16)
            place = place_ref[c : c + 1, :]
            octant = lax.rem(place, 8)
            slot = (
                lax.div(octant, octants) * own
                + lax.rem(octant, octants) * parents
                + lax.div(place, 8)
            )
            code = owner_ref[c] * boxes + slot
            hit = (iota((leaves * boxes, boxes), 0) == code).astype(F32).astype(BF16)
            part = dot(hit, term)
            total = part if total is None else total + part
        for k, block_k in enumerate(blocks128(total.astype(BF16))):
            out_ref[:, k * boxes : (k + 1) * boxes, :] = block_k.reshape(leaves, boxes, LANES)

    pushed = call(
        push_body,
        shape((leaves, leaf_rows, LANES), BF16),
        80_000_000,
        [
            pltpu.VMEM(m2l_ops.shape, BF16),
            pltpu.VMEM(leaf_owner.shape, jnp.int32),
            pltpu.VMEM(leaf_place.shape, jnp.int32),
            pltpu.VMEM((2, 3 * count, LANES), F32),
            pltpu.SemaphoreType.DMA((3,)),
        ],
        [VMEM] * 3 + [HBM] * 3,
        40,
        0,
    )(offsets, vel_cot, shell, *in_hbm(m2l_ops, leaf_owner, leaf_place))

    def pack_body(pushed_ref, *refs):
        *up_refs, out_ref = refs
        total = up_refs[0][...]
        for ref in up_refs[1:]:
            total = total + ref[...]
        out_ref[:, :leaf_rows, :] = pushed_ref[...]
        out_ref[:, leaf_rows:, :] = jnp.broadcast_to(
            total.astype(BF16)[None], (leaves, up_rows, LANES)
        )

    sent = call(
        pack_body, shape((leaves, leaf_rows + up_rows, LANES), BF16), 1_000_000, (), [VMEM] * (1 + lvls)
    )(pushed, *ups)
    got = lax.all_to_all(sent, "leaf", split_axis=0, concat_axis=0, tiled=True)

    def near_body(
        q_ref, dir_ref, offsets_ref, vel_ref, owner_ref, place_ref, near_ref, sel_ref, columns, table, sums
    ):
        mine = lax.axis_index("leaf") * parents
        coarse = leaves * parents
        pick = jnp.concatenate(
            [
                (
                    owner_ref[c] * parents + place_ref[c : c + 1, :]
                    == mine + iota((8, coarse), 0) % parents
                ).astype(F32)
                for c in range(classes)
            ],
            0,
        ).astype(BF16)
        spread = (coarse, leaves * up_rows)
        lane = iota(spread, 1)
        for k in range(pieces):
            expand = (iota(spread, 0) == lane // up_rows * parents + lane % parents) & (
                lane % up_rows // parents == k
            )
            sel_ref[k] = dot(pick, expand.astype(F32).astype(BF16)).astype(BF16)

        left = iota((8, LANES), 1) < per_box
        for j in range(groups):
            lanes = slice(j * LANES, (j + 1) * LANES)
            tile = jnp.concatenate(
                [offsets_ref[:, lanes], vel_ref[:, lanes], jnp.zeros((2, LANES), F32)], 0
            )
            columns[lanes, :] = tile.T
            turned = pltpu.roll(tile, per_box, 1)
            table[2 * j] = jnp.where(left, tile, turned)
            table[2 * j + 1] = jnp.where(left, turned, tile)
        near_ref[...] = jnp.zeros_like(near_ref)
        ones = jnp.ones((8, LANES), BF16)

        def block(j, _):
            for h in range(2):
                box = 2 * j + h
                sources = []
                for n in range(0, slots, 2):
                    codes = [dir_ref[n + i, box] for i in range(2)]
                    moves = [
                        (
                            lax.div(code, 9) - 1,
                            lax.rem(lax.div(code, 3), 3) - 1,
                            lax.rem(code, 3) - 1,
                        )
                        for code in codes
                    ]
                    tile = jnp.where(left, table[q_ref[n, box]], table[q_ref[n + 1, box]])
                    rows = [jnp.broadcast_to(tile[c : c + 1], (8, LANES)) for c in range(6)]
                    for c in range(3):
                        rows[c] = rows[c] + jnp.where(
                            left, moves[0][c].astype(F32), moves[1][c].astype(F32)
                        )
                    sources.append(rows)
                for row in range(0, per_box, 8):
                    tile = columns[pl.ds(pl.multiple_of(box * per_box + row, 8), 8), :]
                    target = [jnp.broadcast_to(tile[:, c : c + 1], (8, LANES)) for c in range(3)]
                    force = None
                    for rows in sources:
                        part = stokeslet([target[c] - rows[c] for c in range(3)], rows[3:])
                        force = part if force is None else [x + y for x, y in zip(force, part)]
                    for c in range(3):
                        sums[c, h * per_box + row : h * per_box + row + 8, :] = force[c]
            p, lvl = lax.div(j, lvls), lax.rem(j, lvls)
            for c in range(3):
                total = dot(ones, sums[c].astype(BF16), NT)
                near_ref[lvl, pl.ds(p * 4 + c, 1), :] = total[0:1]
            return 0

        lax.fori_loop(0, groups, block, 0)

    near, select = call(
        near_body,
        (
            shape((lvls, parents * 4, LANES), F32),
            shape((pieces, 8 * classes, leaves * up_rows), BF16),
        ),
        100_000_000,
        [
            pltpu.VMEM((tall, 8), F32),
            pltpu.VMEM((boxes, 8, LANES), F32),
            pltpu.VMEM((3, LANES, LANES), F32),
        ],
        [SMEM, SMEM] + [VMEM] * 4,
        24,
    )(near_q, near_d, offsets, vel_cot, coarse_owner, coarse_place)

    def mid_body(got_ref, sel_ref, m2l_ref, near_ref, *refs):
        *out_refs, leaf_sum = refs
        me = lax.axis_index("lvl")
        leaf_sum[...] = jnp.sum(got_ref[:, :leaf_rows, :].astype(F32), 0)
        tops = got_ref[:, leaf_rows:, :].reshape(leaves * up_rows, LANES)
        chosen = jnp.concatenate([dot(sel_ref[k], tops) for k in range(pieces)], 1)
        high = chosen.astype(BF16).astype(F32)
        parts = jnp.where(iota(chosen.shape, 0) % 8 < parents, high, chosen - high)
        parts = parts[:, :width].astype(BF16)
        total = dot(parts[0:8], m2l_ref[0])
        for c in range(1, classes):
            total = total + dot(parts[8 * c : 8 * c + 8], m2l_ref[c])
        total = 0.5 * (total[0:parents] + total[parents : 2 * parents])
        total_blocks = blocks128(total)
        for k, out_ref in enumerate(out_refs):
            peer = lax.rem(me + k, lvls)
            for i, block in enumerate(total_blocks):
                out_ref[i * parents : (i + 1) * parents, :] = block.astype(out_ref.dtype)
            for i in range(pieces):
                rows = leaf_sum[pl.ds(pl.multiple_of(i * boxes + peer * own, own), own), :]
                out_ref[up_rows + i * own : up_rows + (i + 1) * own, :] = rows.astype(out_ref.dtype)
            out_ref[up_rows + own_rows :, :] = near_ref[peer].astype(out_ref.dtype)

    pay_rows = up_rows + own_rows + parents * 4
    mids = call(
        mid_body,
        tuple(shape((pay_rows, LANES), BF16 if k else F32) for k in range(lvls)),
        20_000_000,
        [pltpu.VMEM((leaf_rows, LANES), F32)],
        [VMEM] * 4,
    )(got, select, m2l_ops, near)
    mids = [mids[0]] + [shifted(mids[k], k) for k in range(1, lvls)]

    def down_body(child_ref, map_ref, offsets_ref, shell_ref, *refs):
        *mid_refs, out_ref, dens = refs
        me = lax.axis_index("lvl")
        total = mid_refs[0][...]
        for ref in mid_refs[1:]:
            total = total + ref[...].astype(F32)
        top = jnp.concatenate(
            [total[k * parents : (k + 1) * parents] for k in range(pieces)], 1
        )[:, :width].astype(BF16)
        lowered = jnp.concatenate([dot(top, child_ref[o], NT) for o in range(octants)], 0)
        leaf = jnp.concatenate(
            [total[up_rows + k * own : up_rows + (k + 1) * own] for k in range(pieces)], 1
        )[:, :width]
        mult = leaf + lowered
        high = mult.astype(BF16)
        pair = jnp.concatenate([high.astype(F32), mult - high.astype(F32)], 0).astype(BF16)
        mapped = map_ref[...]
        coarse_map = mapped.astype(BF16)
        fine_map = (mapped - coarse_map.astype(F32)).astype(BF16)
        first, second = dot(pair, coarse_map), dot(pair, fine_map)
        check = first[0:own] + first[own:] + second[0:own] + second[own:]
        high = check.astype(BF16).astype(F32)
        pair = jnp.concatenate([high, check - high], 0).astype(BF16)
        here = parents * LANES
        lane = iota((2 * own, here), 1)
        box = lane % LANES // per_box * parents + lane // LANES
        hit = (iota((2 * own, here), 0) % own == box).astype(F32).astype(BF16)
        dens[...] = dot(pair, hit, TN)
        out_ref[...] = total[up_rows + own_rows :]
        for p in range(parents):
            target = rows3(offsets_ref, lanes_of(p, me))
            lanes = slice(p * LANES, (p + 1) * LANES)
            force = [jnp.zeros((8, LANES), F32) for _ in range(3)]
            for row in range(0, count, 8):
                d = [
                    target[c] - shell_ref[c * count + row : c * count + row + 8, :]
                    for c in range(3)
                ]
                q = [dens[c * count + row : c * count + row + 8, lanes] for c in range(3)]
                part = stokeslet(d, q)
                force = [force[c] + part[c] for c in range(3)]
            for c in range(3):
                row = p * 4 + c
                out_ref[row : row + 1, :] += jnp.sum(force[c], 0, keepdims=True)

    forces = call(
        down_body,
        shape((parents * 4, LANES), F32),
        20_000_000,
        [pltpu.VMEM((3 * count, parents * LANES), F32)],
        [VMEM] * (4 + lvls),
    )(child_ops, check_map, offsets, shell, *mids)
    forces = [forces] + [shifted(forces, k) for k in range(1, lvls)]

    def join_body(*refs):
        *parts, out_ref = refs
        me = lax.axis_index("lvl")
        for k, ref in enumerate(parts):
            peer = lax.rem(me + lvls - k, lvls)
            for p in range(parents):
                out_ref[:, lanes_of(p, peer)] = ref[p * 4 : p * 4 + 3, :]

    return call(join_body, shape((3, tall), F32), 100_000, (), [VMEM] * lvls)(*forces)


def solution(mesh):
    placed = (
        P(None, "leaf"),
        P(None, "leaf"),
        P("lvl", None, None),
        P("lvl", None, None),
        P(),
        P("lvl", "leaf", None, None),
        P("lvl", "leaf", None),
        P("lvl", None, None, None),
        P("lvl", None, None),
        P("leaf", "lvl"),
        P("leaf", "lvl"),
    )
    return jax.shard_map(
        local, mesh=mesh, in_specs=placed, out_specs=P(None, "leaf"), check_vma=False
    )
```

```python
import jax
import jax.numpy as jnp
import numpy as np
from jax import lax
from jax.experimental import pallas as pl
from jax.experimental.pallas import tpu as pltpu
from jax.sharding import PartitionSpec as P

SIDE = 6
EPSILON2 = 0.01
RADIUS = 0.525
LANES = 128
F32 = jnp.float32
BF16 = jnp.bfloat16
VMEM = pl.BlockSpec(memory_space=pltpu.VMEM)
HBM = pl.BlockSpec(memory_space=pltpu.HBM)
NN = (((1,), (0,)), ((), ()))
NT = (((1,), (1,)), ((), ()))
TN = (((0,), (0,)), ((), ()))


def surface_points(edge_count):
    levels = np.linspace(-1.0, 1.0, edge_count)
    lattice = np.stack(np.meshgrid(levels, levels, levels, indexing="ij"), 0).reshape(3, -1)
    on_shell = np.max(np.abs(lattice), 0) > 1.0 - 1e-09
    return np.asarray(lattice[:, on_shell] * RADIUS, np.float32)


def dot(a, b, dims=NN):
    return lax.dot_general(a, b, dims, preferred_element_type=F32)


def iota(shape, axis):
    return lax.broadcasted_iota(jnp.int32, shape, axis)


def stokeslet(d, v):
    r2 = d[0] * d[0] + d[1] * d[1] + (d[2] * d[2] + EPSILON2)
    rs = lax.rsqrt(r2)
    weight = rs * (rs * rs)
    scale = rs + EPSILON2 * weight
    along = weight * (d[0] * v[0] + d[1] * v[1] + d[2] * v[2])
    return [scale * v[c] + along * d[c] for c in range(3)]


def call(body, outs, cost, scratch=(), ins=None, vmem=24, touched=1 << 20):
    return pl.pallas_call(
        body,
        out_shape=outs,
        in_specs=ins,
        out_specs=jax.tree.map(lambda _: VMEM, outs),
        scratch_shapes=list(scratch),
        cost_estimate=pl.CostEstimate(flops=cost, bytes_accessed=touched, transcendentals=0),
        compiler_params=pltpu.CompilerParams(vmem_limit_bytes=vmem << 20),
    )


def in_hbm(*arrays):
    return [pltpu.with_memory_space_constraint(array, pltpu.HBM) for array in arrays]


def start_all(sources, targets, sems):
    copies = [
        pltpu.make_async_copy(source, target, sems.at[i])
        for i, (source, target) in enumerate(zip(sources, targets))
    ]
    for copy in copies:
        copy.start()
    return copies


def held(*arrays):
    return [pltpu.VMEM(array.shape, array.dtype) for array in arrays]


def shape(dims, dtype):
    return jax.ShapeDtypeStruct(tuple(dims), dtype)


def surface_block(points, vectors, shell_ref, fields, column):
    count = shell_ref.shape[0] // 3
    for row in range(0, count, 8):
        spots = [slice(c * count + row, c * count + row + 8) for c in range(3)]
        d = [shell_ref[spots[c], :] - points[c] for c in range(3)]
        for c, value in enumerate(stokeslet(d, vectors)):
            fields[spots[c], column] = value


def blocks128(matrix):
    width = matrix.shape[1]
    fill = -width % LANES
    if fill:
        matrix = jnp.concatenate([matrix, jnp.zeros((matrix.shape[0], fill), matrix.dtype)], 1)
    return [matrix[:, k : k + LANES] for k in range(0, width, LANES)]


def local(
    offsets,
    vel_cot,
    m2l_ops,
    child_ops,
    check_map,
    leaf_dest,
    leaf_slot,
    coarse_dest,
    coarse_slot,
    near_box,
    near_dir,
):
    shell_np = surface_points(SIDE)
    count = shell_np.shape[1]
    width = m2l_ops.shape[1]
    classes = m2l_ops.shape[0]
    octants = child_ops.shape[0]
    boxes, slots = near_box.shape
    per_box = offsets.shape[1] // boxes
    parents = boxes // 8
    own = parents * octants
    leaves = lax.axis_size("leaf")
    lvls = lax.axis_size("lvl")
    pieces = -(-width // LANES)
    group = octants * per_box
    groups = parents * lvls
    assert group == LANES and own == 8 and parents == 4 and lvls * octants == 8
    up_rows = pieces * parents
    leaf_rows = pieces * boxes
    own_rows = pieces * own
    tall = groups * LANES
    shell = jnp.asarray(np.repeat(shell_np.reshape(-1, 1), LANES, 1))

    leaf_owner = leaf_dest.transpose(0, 2, 3, 1)[0]
    leaf_place = leaf_slot.transpose(0, 2, 1)[0]
    coarse_owner = coarse_dest.transpose(0, 2, 3, 1)[0]
    coarse_place = coarse_slot.transpose(0, 2, 1)[0]
    near_q = near_box.T
    near_d = near_dir.T

    def lanes_of(parent, lvl):
        return pl.ds(pl.multiple_of((parent * lvls + lvl) * LANES, LANES), LANES)

    def box_row(octant, box):
        return lax.rem(octant, octants) * parents + lax.div(box, 8)

    def rows3(ref, lanes):
        return [ref[c : c + 1, lanes] for c in range(3)]

    def up_body(
        offsets_hbm,
        vel_hbm,
        shell_hbm,
        owner_hbm,
        place_hbm,
        child_hbm,
        sent_ref,
        offsets_ref,
        vel_ref,
        shell_ref,
        owner_ref,
        place_ref,
        child_ref,
        fields,
        slot_ref,
        sems,
    ):
        me = lax.axis_index("lvl")
        copies = start_all(
            (offsets_hbm, vel_hbm, shell_hbm, owner_hbm, place_hbm, child_hbm),
            (offsets_ref, vel_ref, shell_ref, owner_ref, place_ref, child_ref),
            sems,
        )
        for copy in copies[:5]:
            copy.wait()
        for p in range(parents):
            lanes = lanes_of(p, me)
            surface_block(
                rows3(offsets_ref, lanes),
                rows3(vel_ref, lanes),
                shell_ref,
                fields,
                slice(p * LANES, (p + 1) * LANES),
            )
        place = jnp.concatenate([place_ref[...], place_ref[...]], 0)
        octant = lax.rem(place, 8)
        spot = lax.div(octant, octants) * own + box_row(octant, place)
        owner = jnp.concatenate(
            [owner_ref[c] for c in range(classes)] + [jnp.zeros((classes, boxes), jnp.int32)], 0
        )
        ids = jnp.where(iota((2 * classes, boxes), 0) < classes, owner, spot)
        box = iota((boxes, LANES), 0)
        octant = lax.rem(box, 8)
        spot = lax.div(octant, octants) * own + box_row(octant, box)
        moved = iota((boxes, LANES), 1) == LANES - boxes + spot
        ids = dot(ids.astype(F32).astype(BF16), moved.astype(F32).astype(BF16))

        here = parents * LANES
        lane = iota((own + 8 * octants, here), 1)
        row = iota((own + 8 * octants, here), 0)
        second, p = (lane % LANES) // per_box, lane // LANES
        target = jnp.where(row < own, second * parents + p, own + second * 8 + p)
        pick = (row == target).astype(F32).astype(BF16)
        leaf = dot(pick, fields[...].astype(BF16), NT)
        for k, block in enumerate(blocks128(leaf[0:own])):
            slot_ref[k * own : (k + 1) * own, :] = block + (ids if k == pieces - 1 else 0.0)
        leaf = leaf.astype(BF16)
        copies[5].wait()
        total = None
        for o in range(octants):
            part = dot(leaf[own + 8 * o : own + 8 * o + 8], child_ref[o])
            total = part if total is None else total + part
        for k, block in enumerate(blocks128(total)):
            first = own_rows + k * parents
            slot_ref[first : first + parents, :] = block[0:parents]
        sent_ref[...] = jnp.broadcast_to(slot_ref[...].astype(BF16)[None], sent_ref.shape)

    slot_rows = own_rows + up_rows
    devices = leaves * lvls
    up_inputs = (offsets, vel_cot, shell, leaf_owner, leaf_place, child_ops)
    sent = call(
        up_body,
        shape((devices, slot_rows, LANES), BF16),
        20_000_000,
        held(*up_inputs)
        + [
            pltpu.VMEM((3 * count, parents * LANES), F32),
            pltpu.VMEM((slot_rows, LANES), F32),
            pltpu.SemaphoreType.DMA((6,)),
        ],
        [HBM] * 6,
        40,
    )(*in_hbm(*up_inputs))
    got = lax.all_to_all(sent, ("leaf", "lvl"), split_axis=0, concat_axis=0, tiled=True)

    def shifted(value, k):
        return lax.ppermute(value, "lvl", [(i, (i + k) % lvls) for i in range(lvls)])

    def near_body(*refs):
        sources, (near_ref, sel_ref), targets = refs[:6], refs[6:8], refs[8:14]
        columns, table, sums, sems = refs[14:]
        q_ref, dir_ref, offsets_ref, vel_ref, owner_ref, place_ref = targets
        for copy in start_all(sources, targets, sems):
            copy.wait()
        mine = lax.axis_index("leaf") * parents
        coarse = leaves * parents
        pick = jnp.concatenate(
            [
                (
                    owner_ref[c] * parents + place_ref[c : c + 1, :]
                    == mine + iota((8, coarse), 0) % parents
                ).astype(F32)
                for c in range(classes)
            ],
            0,
        ).astype(BF16)
        spread = (coarse, leaves * up_rows)
        lane = iota(spread, 1)
        for k in range(pieces):
            expand = (iota(spread, 0) == lane // up_rows * parents + lane % parents) & (
                lane % up_rows // parents == k
            )
            sel_ref[k] = dot(pick, expand.astype(F32).astype(BF16)).astype(BF16)

        left = iota((8, LANES), 1) < per_box
        for j in range(groups):
            lanes = slice(j * LANES, (j + 1) * LANES)
            tile = jnp.concatenate(
                [offsets_ref[:, lanes], vel_ref[:, lanes], jnp.zeros((2, LANES), F32)], 0
            )
            columns[lanes, :] = tile.T
            turned = pltpu.roll(tile, per_box, 1)
            table[2 * j] = jnp.where(left, tile, turned)
            table[2 * j + 1] = jnp.where(left, turned, tile)
        near_ref[...] = jnp.zeros_like(near_ref)
        ones = jnp.ones((8, LANES), BF16)

        def block(j, _):
            for h in range(2):
                box = 2 * j + h
                sources = []
                for n in range(0, slots, 2):
                    codes = [dir_ref[n + i, box] for i in range(2)]
                    moves = [
                        (
                            lax.div(code, 9) - 1,
                            lax.rem(lax.div(code, 3), 3) - 1,
                            lax.rem(code, 3) - 1,
                        )
                        for code in codes
                    ]
                    tile = jnp.where(left, table[q_ref[n, box]], table[q_ref[n + 1, box]])
                    rows = [jnp.broadcast_to(tile[c : c + 1], (8, LANES)) for c in range(6)]
                    for c in range(3):
                        rows[c] = rows[c] + jnp.where(
                            left, moves[0][c].astype(F32), moves[1][c].astype(F32)
                        )
                    sources.append(rows)
                for row in range(0, per_box, 8):
                    tile = columns[pl.ds(pl.multiple_of(box * per_box + row, 8), 8), :]
                    target = [jnp.broadcast_to(tile[:, c : c + 1], (8, LANES)) for c in range(3)]
                    force = None
                    for rows in sources:
                        part = stokeslet([target[c] - rows[c] for c in range(3)], rows[3:])
                        force = part if force is None else [x + y for x, y in zip(force, part)]
                    for c in range(3):
                        sums[c, h * per_box + row : h * per_box + row + 8, :] = force[c]
            p, lvl = lax.div(j, lvls), lax.rem(j, lvls)
            for c in range(3):
                total = dot(ones, sums[c].astype(BF16), NT)
                near_ref[lvl, pl.ds(p * 4 + c, 1), :] = total[0:1]
            return 0

        lax.fori_loop(0, groups, block, 0)

    near, select = call(
        near_body,
        (
            shape((lvls, parents * 4, LANES), F32),
            shape((pieces, 8 * classes, leaves * up_rows), BF16),
        ),
        100_000_000,
        [pltpu.SMEM(near_q.shape, jnp.int32), pltpu.SMEM(near_d.shape, jnp.int32)]
        + held(offsets, vel_cot, coarse_owner, coarse_place)
        + [
            pltpu.VMEM((tall, 8), F32),
            pltpu.VMEM((boxes, 8, LANES), F32),
            pltpu.VMEM((3, LANES, LANES), F32),
            pltpu.SemaphoreType.DMA((6,)),
        ],
        [HBM] * 6,
        24,
    )(*in_hbm(near_q, near_d, offsets, vel_cot, coarse_owner, coarse_place))

    def mid_body(got_ref, sel_ref, m2l_ref, near_ref, *refs):
        *out_refs, leaf_sum = refs
        me = lax.axis_index("lvl")
        mine = lax.axis_index("leaf").astype(F32)
        tops = got_ref[:, own_rows:, :].astype(F32).reshape(leaves, lvls, up_rows, LANES)
        tops = jnp.sum(tops, 1).astype(BF16).reshape(leaves * up_rows, LANES)
        chosen = jnp.concatenate([dot(sel_ref[k], tops) for k in range(pieces)], 1)
        high = chosen.astype(BF16).astype(F32)
        parts = jnp.where(iota(chosen.shape, 0) % 8 < parents, high, chosen - high)

        per_tile = LANES // boxes
        lane = iota((2 * classes, LANES), 1)
        ids = []
        for first in range(0, leaves, per_tile):
            tile = jnp.zeros((2 * classes, LANES), F32)
            for i in range(min(per_tile, leaves - first)):
                piece = got_ref[(first + i) * lvls + me, own_rows - own : own_rows, :].astype(F32)
                piece = pltpu.roll(piece, (i + 1) * boxes % LANES, 1)
                tile = jnp.where(lax.div(lane, boxes) == i, piece, tile)
            ids.append(tile)
        ids = jnp.concatenate(ids, 1)[:, : leaves * boxes]
        row = iota((boxes, leaves * boxes), 0).astype(F32)
        hits = jnp.concatenate(
            [
                ((ids[c : c + 1] == mine) & (ids[classes + c : classes + c + 1] == row)).astype(F32)
                for c in range(classes)
            ],
            0,
        ).astype(BF16)
        gathered = jnp.concatenate(
            [
                dot(hits, got_ref[:, k * own : (k + 1) * own, :].reshape(devices * own, LANES))
                for k in range(pieces)
            ],
            1,
        )
        total = None
        for c in range(classes):
            rows = jnp.concatenate(
                [gathered[c * boxes : (c + 1) * boxes], parts[8 * c : 8 * c + 8]], 0
            )
            part = dot(rows[:, :width].astype(BF16), m2l_ref[c])
            total = part if total is None else total + part
        for k, block in enumerate(blocks128(total[:boxes])):
            leaf_sum[k * boxes : (k + 1) * boxes, :] = block
        total = total[boxes:]
        total = 0.5 * (total[0:parents] + total[parents : 2 * parents])
        total_blocks = blocks128(total)
        for k, out_ref in enumerate(out_refs):
            peer = lax.rem(me + k, lvls)
            for i, block in enumerate(total_blocks):
                out_ref[i * parents : (i + 1) * parents, :] = block.astype(out_ref.dtype)
            for i in range(pieces):
                rows = leaf_sum[pl.ds(pl.multiple_of(i * boxes + peer * own, own), own), :]
                out_ref[up_rows + i * own : up_rows + (i + 1) * own, :] = rows.astype(out_ref.dtype)
            out_ref[up_rows + own_rows :, :] = near_ref[peer].astype(out_ref.dtype)

    pay_rows = up_rows + own_rows + parents * 4
    mids = call(
        mid_body,
        tuple(shape((pay_rows, LANES), BF16 if k else F32) for k in range(lvls)),
        20_000_000,
        [pltpu.VMEM((leaf_rows, LANES), F32)],
        [VMEM] * 4,
        40,
    )(got, select, m2l_ops, near)
    mids = [mids[0]] + [shifted(mids[k], k) for k in range(1, lvls)]

    def down_body(child_ref, map_ref, offsets_ref, shell_ref, *refs):
        *mid_refs, out_ref, dens = refs
        me = lax.axis_index("lvl")
        total = mid_refs[0][...]
        for ref in mid_refs[1:]:
            total = total + ref[...].astype(F32)
        top = jnp.concatenate(
            [total[k * parents : (k + 1) * parents] for k in range(pieces)], 1
        )[:, :width].astype(BF16)
        lowered = jnp.concatenate([dot(top, child_ref[o], NT) for o in range(octants)], 0)
        leaf = jnp.concatenate(
            [total[up_rows + k * own : up_rows + (k + 1) * own] for k in range(pieces)], 1
        )[:, :width]
        mult = leaf + lowered
        high = mult.astype(BF16)
        pair = jnp.concatenate([high.astype(F32), mult - high.astype(F32)], 0).astype(BF16)
        mapped = map_ref[...]
        coarse_map = mapped.astype(BF16)
        fine_map = (mapped - coarse_map.astype(F32)).astype(BF16)
        first, second = dot(pair, coarse_map), dot(pair, fine_map)
        check = first[0:own] + first[own:] + second[0:own] + second[own:]
        high = check.astype(BF16).astype(F32)
        pair = jnp.concatenate([high, check - high], 0).astype(BF16)
        here = parents * LANES
        lane = iota((2 * own, here), 1)
        box = lane % LANES // per_box * parents + lane // LANES
        hit = (iota((2 * own, here), 0) % own == box).astype(F32).astype(BF16)
        dens[...] = dot(pair, hit, TN)
        out_ref[...] = total[up_rows + own_rows :]
        for p in range(parents):
            target = rows3(offsets_ref, lanes_of(p, me))
            lanes = slice(p * LANES, (p + 1) * LANES)
            force = [jnp.zeros((8, LANES), F32) for _ in range(3)]
            for row in range(0, count, 8):
                d = [
                    target[c] - shell_ref[c * count + row : c * count + row + 8, :]
                    for c in range(3)
                ]
                q = [dens[c * count + row : c * count + row + 8, lanes] for c in range(3)]
                part = stokeslet(d, q)
                force = [force[c] + part[c] for c in range(3)]
            for c in range(3):
                row = p * 4 + c
                out_ref[row : row + 1, :] += jnp.sum(force[c], 0, keepdims=True)

    forces = call(
        down_body,
        shape((parents * 4, LANES), F32),
        20_000_000,
        [pltpu.VMEM((3 * count, parents * LANES), F32)],
        [VMEM] * (4 + lvls),
    )(child_ops, check_map, offsets, shell, *mids)
    forces = [forces] + [shifted(forces, k) for k in range(1, lvls)]

    def join_body(*refs):
        *parts, out_ref = refs
        me = lax.axis_index("lvl")
        for k, ref in enumerate(parts):
            peer = lax.rem(me + lvls - k, lvls)
            for p in range(parents):
                out_ref[:, lanes_of(p, peer)] = ref[p * 4 : p * 4 + 3, :]

    return call(join_body, shape((3, tall), F32), 100_000, (), [VMEM] * lvls)(*forces)


def solution(mesh):
    placed = (
        P(None, "leaf"),
        P(None, "leaf"),
        P("lvl", None, None),
        P("lvl", None, None),
        P(),
        P("lvl", "leaf", None, None),
        P("lvl", "leaf", None),
        P("lvl", None, None, None),
        P("lvl", None, None),
        P("leaf", "lvl"),
        P("leaf", "lvl"),
    )
    return jax.shard_map(
        local, mesh=mesh, in_specs=placed, out_specs=P(None, "leaf"), check_vma=False
    )
```

```python
import jax
import jax.numpy as jnp
import numpy as np
from jax import lax
from jax.experimental import pallas as pl
from jax.experimental.pallas import tpu as pltpu
from jax.sharding import PartitionSpec as P

SIDE = 6
EPSILON2 = 0.01
RADIUS = 0.525
LANES = 128
F32 = jnp.float32
BF16 = jnp.bfloat16
VMEM = pl.BlockSpec(memory_space=pltpu.VMEM)
HBM = pl.BlockSpec(memory_space=pltpu.HBM)
NN = (((1,), (0,)), ((), ()))
NT = (((1,), (1,)), ((), ()))
TN = (((0,), (0,)), ((), ()))


def surface_points(edge_count):
    levels = np.linspace(-1.0, 1.0, edge_count)
    lattice = np.stack(np.meshgrid(levels, levels, levels, indexing="ij"), 0).reshape(3, -1)
    on_shell = np.max(np.abs(lattice), 0) > 1.0 - 1e-09
    return np.asarray(lattice[:, on_shell] * RADIUS, np.float32)


def dot(a, b, dims=NN):
    return lax.dot_general(a, b, dims, preferred_element_type=F32)


def iota(shape, axis):
    return lax.broadcasted_iota(jnp.int32, shape, axis)


def stokeslet(d, v):
    r2 = d[0] * d[0] + d[1] * d[1] + (d[2] * d[2] + EPSILON2)
    rs = lax.rsqrt(r2)
    weight = rs * (rs * rs)
    scale = rs + EPSILON2 * weight
    along = weight * (d[0] * v[0] + d[1] * v[1] + d[2] * v[2])
    return [scale * v[c] + along * d[c] for c in range(3)]


def call(body, outs, cost, scratch=(), ins=None, vmem=24, spec=VMEM):
    return pl.pallas_call(
        body,
        out_shape=outs,
        in_specs=ins,
        out_specs=jax.tree.map(lambda _: spec, outs),
        scratch_shapes=list(scratch),
        cost_estimate=pl.CostEstimate(flops=cost, bytes_accessed=1 << 20, transcendentals=0),
        compiler_params=pltpu.CompilerParams(vmem_limit_bytes=vmem << 20),
    )


def in_hbm(*arrays):
    return [pltpu.with_memory_space_constraint(array, pltpu.HBM) for array in arrays]


def start_all(sources, targets, sems):
    copies = [
        pltpu.make_async_copy(source, target, sems.at[i])
        for i, (source, target) in enumerate(zip(sources, targets))
    ]
    for copy in copies:
        copy.start()
    return copies


def held(*arrays):
    return [pltpu.VMEM(array.shape, array.dtype) for array in arrays]


def shape(dims, dtype):
    return jax.ShapeDtypeStruct(tuple(dims), dtype)


def surface_block(points, vectors, shell_ref, fields, column):
    count = shell_ref.shape[0] // 3
    for row in range(0, count, 8):
        spots = [slice(c * count + row, c * count + row + 8) for c in range(3)]
        d = [shell_ref[spots[c], :] - points[c] for c in range(3)]
        for c, value in enumerate(stokeslet(d, vectors)):
            fields[spots[c], column] = value


def blocks128(matrix):
    width = matrix.shape[1]
    fill = -width % LANES
    if fill:
        matrix = jnp.concatenate([matrix, jnp.zeros((matrix.shape[0], fill), matrix.dtype)], 1)
    return [matrix[:, k : k + LANES] for k in range(0, width, LANES)]


def local(
    offsets,
    vel_cot,
    m2l_ops,
    child_ops,
    check_map,
    leaf_dest,
    leaf_slot,
    coarse_dest,
    coarse_slot,
    near_box,
    near_dir,
):
    shell_np = surface_points(SIDE)
    count = shell_np.shape[1]
    width = m2l_ops.shape[1]
    classes = m2l_ops.shape[0]
    octants = child_ops.shape[0]
    boxes, slots = near_box.shape
    per_box = offsets.shape[1] // boxes
    parents = boxes // 8
    own = parents * octants
    leaves = lax.axis_size("leaf")
    lvls = lax.axis_size("lvl")
    pieces = -(-width // LANES)
    group = octants * per_box
    groups = parents * lvls
    assert group == LANES and own == 8 and parents == 4 and lvls * octants == 8
    assert octants == 2 and classes == parents and pieces == 4 and lvls % 2 == 0
    ids_lanes = boxes // 2
    assert width + 2 * ids_lanes <= pieces * LANES
    up_rows = pieces * parents
    leaf_rows = pieces * boxes
    own_rows = pieces * own
    tall = groups * LANES
    shell = jnp.asarray(np.repeat(shell_np.reshape(-1, 1), LANES, 1))

    leaf_owner = leaf_dest.transpose(0, 2, 3, 1)[0]
    leaf_place = leaf_slot.transpose(0, 2, 1)[0]
    coarse_owner = coarse_dest.transpose(0, 2, 3, 1)[0]
    coarse_place = coarse_slot.transpose(0, 2, 1)[0]
    near_q = near_box.T
    near_d = near_dir.T

    def lanes_of(parent, lvl):
        return pl.ds(pl.multiple_of((parent * lvls + lvl) * LANES, LANES), LANES)

    def box_row(octant, box):
        return lax.rem(octant, octants) * parents + lax.div(box, 8)

    def rows3(ref, lanes):
        return [ref[c : c + 1, lanes] for c in range(3)]

    def up_body(
        offsets_hbm,
        vel_hbm,
        shell_hbm,
        owner_hbm,
        place_hbm,
        child_hbm,
        sent_ref,
        offsets_ref,
        vel_ref,
        shell_ref,
        owner_ref,
        place_ref,
        child_ref,
        fields,
        slot_ref,
        slots_ref,
        sems,
    ):
        me = lax.axis_index("lvl")
        copies = start_all(
            (offsets_hbm, vel_hbm, shell_hbm, owner_hbm, place_hbm, child_hbm),
            (offsets_ref, vel_ref, shell_ref, owner_ref, place_ref, child_ref),
            sems,
        )
        for copy in copies[:5]:
            copy.wait()
        for p in range(parents):
            lanes = lanes_of(p, me)
            surface_block(
                rows3(offsets_ref, lanes),
                rows3(vel_ref, lanes),
                shell_ref,
                fields,
                slice(p * LANES, (p + 1) * LANES),
            )
        place = place_ref[...]
        octant = lax.rem(place, 8)
        spot = lax.div(octant, octants) * own + box_row(octant, place)
        spot = spot.astype(F32).astype(BF16)
        owner = jnp.concatenate([owner_ref[c] for c in range(classes)], 0).astype(F32).astype(BF16)
        box = iota((boxes, LANES), 0)
        octant = lax.rem(box, 8)
        lane = iota((boxes, LANES), 1)
        spread = lax.div(octant, octants) * parents + lax.div(box, 8)
        ids = []
        for half in range(2):
            kept = lax.rem(octant, 2) == half
            first = kept & (lane == spread + (LANES - 2 * ids_lanes))
            second = kept & (lane == spread + (LANES - ids_lanes))
            ids.append(
                dot(owner, first.astype(F32).astype(BF16))
                + dot(spot, second.astype(F32).astype(BF16))
            )

        here = parents * LANES
        lane = iota((own + 8 * octants, here), 1)
        row = iota((own + 8 * octants, here), 0)
        second, p = (lane % LANES) // per_box, lane // LANES
        target = jnp.where(row < own, second * parents + p, own + second * 8 + p)
        pick = (row == target).astype(F32).astype(BF16)
        leaf = dot(pick, fields[...].astype(BF16), NT)
        for k, block in enumerate(blocks128(leaf[0:own])):
            for half in range(2):
                rows = block[half * parents : (half + 1) * parents]
                slot_ref[half, k * parents : (k + 1) * parents, :] = (
                    rows + ids[half] if k == pieces - 1 else rows
                )
        leaf = leaf.astype(BF16)
        copies[5].wait()
        total = None
        for o in range(octants):
            part = dot(leaf[own + 8 * o : own + 8 * o + 8], child_ref[o])
            total = part if total is None else total + part
        for k, block in enumerate(blocks128(total)):
            for half in range(2):
                first = up_rows + k * parents
                slot_ref[half, first : first + parents, :] = block[0:parents]
        slots_ref[...] = jnp.broadcast_to(
            slot_ref[...].astype(BF16)[None], (devices // 2, 2, slot_rows, LANES)
        ).reshape(slots_ref.shape)
        copy = pltpu.make_async_copy(slots_ref, sent_ref, sems.at[6])
        copy.start()
        copy.wait()

    slot_rows = 2 * up_rows
    devices = leaves * lvls
    up_inputs = (offsets, vel_cot, shell, leaf_owner, leaf_place, child_ops)
    sent = call(
        up_body,
        pltpu.HBM((devices, slot_rows, LANES), BF16),
        20_000_000,
        held(*up_inputs)
        + [
            pltpu.VMEM((3 * count, parents * LANES), F32),
            pltpu.VMEM((2, slot_rows, LANES), F32),
            pltpu.VMEM((devices, slot_rows, LANES), BF16),
            pltpu.SemaphoreType.DMA((7,)),
        ],
        [HBM] * 6,
        40,
        HBM,
    )(*in_hbm(*up_inputs))
    got = lax.all_to_all(sent, ("leaf", "lvl"), split_axis=0, concat_axis=0, tiled=True)

    def exchanged(values):
        peers = []
        for k in range(1, lvls):
            peers.append(lax.ppermute(values[k], "lvl", [(i, i ^ k) for i in range(lvls)]))
        return [values[0]] + peers

    pair_ops = lax.ppermute(m2l_ops, "lvl", [(i, i ^ 1) for i in range(lvls)])

    def near_body(*refs):
        sources, pair_hbm, (near_ref, sel_ref, head_ref) = refs[:6], refs[6], refs[7:10]
        targets = refs[10:16]
        columns, table, sums, sems = refs[16:]
        q_ref, dir_ref, offsets_ref, vel_ref, owner_ref, place_ref = targets
        *copies, head_copy = start_all(
            (*sources, pair_hbm.at[: head_ref.shape[0]]), (*targets, head_ref), sems
        )
        for copy in copies:
            copy.wait()
        mine = lax.axis_index("leaf") * parents
        coarse = leaves * parents
        pick = jnp.concatenate(
            [
                (
                    owner_ref[c] * parents + place_ref[c : c + 1, :]
                    == mine + iota((8, coarse), 0) % parents
                ).astype(F32)
                for c in range(classes)
            ],
            0,
        ).astype(BF16)
        spread = (coarse, leaves * up_rows)
        lane = iota(spread, 1)
        for k in range(pieces):
            expand = (iota(spread, 0) == lane // up_rows * parents + lane % parents) & (
                lane % up_rows // parents == k
            )
            sel_ref[k] = dot(pick, expand.astype(F32).astype(BF16)).astype(BF16)

        left = iota((8, LANES), 1) < per_box
        for j in range(groups):
            lanes = slice(j * LANES, (j + 1) * LANES)
            tile = jnp.concatenate(
                [offsets_ref[:, lanes], vel_ref[:, lanes], jnp.zeros((2, LANES), F32)], 0
            )
            columns[lanes, :] = tile.T
            turned = pltpu.roll(tile, per_box, 1)
            table[2 * j] = jnp.where(left, tile, turned)
            table[2 * j + 1] = jnp.where(left, turned, tile)
        near_ref[...] = jnp.zeros_like(near_ref)
        ones = jnp.ones((8, LANES), BF16)

        def block(j, _):
            for h in range(2):
                box = 2 * j + h
                sources = []
                for n in range(0, slots, 2):
                    codes = [dir_ref[n + i, box] for i in range(2)]
                    moves = [
                        (
                            lax.div(code, 9) - 1,
                            lax.rem(lax.div(code, 3), 3) - 1,
                            lax.rem(code, 3) - 1,
                        )
                        for code in codes
                    ]
                    tile = jnp.where(left, table[q_ref[n, box]], table[q_ref[n + 1, box]])
                    rows = [jnp.broadcast_to(tile[c : c + 1], (8, LANES)) for c in range(6)]
                    for c in range(3):
                        rows[c] = rows[c] + jnp.where(
                            left, moves[0][c].astype(F32), moves[1][c].astype(F32)
                        )
                    sources.append(rows)
                for row in range(0, per_box, 8):
                    tile = columns[pl.ds(pl.multiple_of(box * per_box + row, 8), 8), :]
                    target = [jnp.broadcast_to(tile[:, c : c + 1], (8, LANES)) for c in range(3)]
                    force = None
                    for rows in sources:
                        part = stokeslet([target[c] - rows[c] for c in range(3)], rows[3:])
                        force = part if force is None else [x + y for x, y in zip(force, part)]
                    for c in range(3):
                        sums[c, h * per_box + row : h * per_box + row + 8, :] = force[c]
            p, lvl = lax.div(j, lvls), lax.rem(j, lvls)
            for c in range(3):
                total = dot(ones, sums[c].astype(BF16), NT)
                near_ref[lvl, pl.ds(p * 4 + c, 1), :] = total[0:1]
            return 0

        lax.fori_loop(0, groups, block, 0)
        head_copy.wait()

    heads = 2
    near, select, pair_head = call(
        near_body,
        (
            shape((lvls, parents * 4, LANES), F32),
            shape((pieces, 8 * classes, leaves * up_rows), BF16),
            shape((heads, width, width), BF16),
        ),
        100_000_000,
        [pltpu.SMEM(near_q.shape, jnp.int32), pltpu.SMEM(near_d.shape, jnp.int32)]
        + held(offsets, vel_cot, coarse_owner, coarse_place)
        + [
            pltpu.VMEM((tall, 8), F32),
            pltpu.VMEM((boxes, 8, LANES), F32),
            pltpu.VMEM((3, LANES, LANES), F32),
            pltpu.SemaphoreType.DMA((7,)),
        ],
        [HBM] * 7,
        24,
    )(*in_hbm(near_q, near_d, offsets, vel_cot, coarse_owner, coarse_place, pair_ops))

    def mid_body(got_ref, sel_ref, m2l_ref, near_ref, head_ref, pair_hbm, *refs):
        *out_refs, tail_ref, leaf_sum, sem = refs
        copy = pltpu.make_async_copy(pair_hbm.at[heads:], tail_ref, sem)
        copy.start()
        me = lax.axis_index("lvl")
        mine = lax.axis_index("leaf").astype(F32)
        tops = got_ref[:, up_rows:, :].astype(F32).reshape(leaves, lvls, up_rows, LANES)
        tops = jnp.sum(tops, 1).astype(BF16).reshape(leaves * up_rows, LANES)
        chosen = jnp.concatenate([dot(sel_ref[k], tops) for k in range(pieces)], 1)
        high = chosen.astype(BF16).astype(F32)
        parts = jnp.where(iota(chosen.shape, 0) % 8 < parents, high, chosen - high)

        tile = (2 * classes, LANES)
        lane, row = iota(tile, 1), iota(tile, 0)
        doubled = iota((LANES, 2 * LANES), 1)
        doubled = iota((LANES, 2 * LANES), 0) == lax.div(doubled, 8) * 4 + lax.rem(doubled, 4)
        doubled = doubled.astype(F32).astype(BF16)
        other = me + 1 - 2 * lax.rem(me, 2)
        last = slice(up_rows - 8, up_rows)
        ids = []
        for first in range(0, leaves, LANES // ids_lanes):
            owner = spot = jnp.zeros(tile, F32)
            for i in range(min(LANES // ids_lanes, leaves - first)):
                at = (first + i) * lvls
                piece = jnp.where(
                    row < classes,
                    pltpu.roll(got_ref[at + me, last, :].astype(F32), 4, 0),
                    got_ref[at + other, last, :].astype(F32),
                )
                here = lax.div(lane, ids_lanes) == i
                owner = jnp.where(here, pltpu.roll(piece, (i + 2) * ids_lanes % LANES, 1), owner)
                spot = jnp.where(here, pltpu.roll(piece, (i + 1) * ids_lanes % LANES, 1), spot)
            ids.append(dot(jnp.concatenate([owner, spot], 0).astype(BF16), doubled))
        ids = jnp.concatenate(ids, 1)[:, : devices * 8]
        spots = iota((boxes, devices * 8), 0).astype(F32)
        hits = jnp.concatenate(
            [
                (
                    (ids[c : c + 1] == mine) & (ids[2 * classes + c : 2 * classes + c + 1] == spots)
                ).astype(F32)
                for c in range(2 * classes)
            ],
            0,
        )
        upper = iota(hits.shape, 1) % 8 < 4
        hits = [jnp.where(upper, hits, 0.0).astype(BF16), jnp.where(upper, 0.0, hits).astype(BF16)]
        gathered = jnp.concatenate(
            [
                dot(hits[k % 2], got_ref[:, k // 2 * 8 : k // 2 * 8 + 8, :].reshape(devices * 8, LANES))
                for k in range(pieces)
            ],
            1,
        )[:, :width]
        total = None
        for c in range(classes):
            rows = jnp.concatenate(
                [gathered[c * boxes : (c + 1) * boxes], parts[8 * c : 8 * c + 8, :width]], 0
            )
            part = dot(rows.astype(BF16), m2l_ref[c])
            total = part if total is None else total + part
        leaf = total[:boxes]
        for c in range(classes):
            if c == heads:
                copy.wait()
            rows = gathered[(classes + c) * boxes : (classes + c + 1) * boxes]
            leaf = leaf + dot(rows.astype(BF16), head_ref[c] if c < heads else tail_ref[c - heads])
        for k, block in enumerate(blocks128(leaf)):
            leaf_sum[k * boxes : (k + 1) * boxes, :] = block
        total = total[boxes:]
        total = 0.5 * (total[0:parents] + total[parents : 2 * parents])
        total_blocks = blocks128(total)
        for k, out_ref in enumerate(out_refs):
            peer = jnp.bitwise_xor(me, k)
            for i, block in enumerate(total_blocks):
                out_ref[i * parents : (i + 1) * parents, :] = block.astype(out_ref.dtype)
            for i in range(pieces):
                rows = leaf_sum[pl.ds(pl.multiple_of(i * boxes + peer * own, own), own), :]
                out_ref[up_rows + i * own : up_rows + (i + 1) * own, :] = rows.astype(out_ref.dtype)
            out_ref[up_rows + own_rows :, :] = near_ref[peer].astype(out_ref.dtype)

    pay_rows = up_rows + own_rows + parents * 4
    mids = call(
        mid_body,
        tuple(shape((pay_rows, LANES), BF16 if k else F32) for k in range(lvls)),
        20_000_000,
        [
            pltpu.VMEM((classes - heads, width, width), BF16),
            pltpu.VMEM((leaf_rows, LANES), F32),
            pltpu.SemaphoreType.DMA,
        ],
        [VMEM] * 5 + [HBM],
        40,
    )(got, select, m2l_ops, near, pair_head, *in_hbm(pair_ops))
    mids = exchanged(mids)

    def down_body(child_ref, map_ref, offsets_ref, shell_ref, *refs):
        *mid_refs, out_ref, dens = refs
        me = lax.axis_index("lvl")
        total = mid_refs[0][...]
        for ref in mid_refs[1:]:
            total = total + ref[...].astype(F32)
        top = jnp.concatenate(
            [total[k * parents : (k + 1) * parents] for k in range(pieces)], 1
        )[:, :width].astype(BF16)
        lowered = jnp.concatenate([dot(top, child_ref[o], NT) for o in range(octants)], 0)
        leaf = jnp.concatenate(
            [total[up_rows + k * own : up_rows + (k + 1) * own] for k in range(pieces)], 1
        )[:, :width]
        mult = leaf + lowered
        high = mult.astype(BF16)
        pair = jnp.concatenate([high.astype(F32), mult - high.astype(F32)], 0).astype(BF16)
        mapped = map_ref[...]
        coarse_map = mapped.astype(BF16)
        fine_map = (mapped - coarse_map.astype(F32)).astype(BF16)
        first, second = dot(pair, coarse_map), dot(pair, fine_map)
        check = first[0:own] + first[own:] + second[0:own] + second[own:]
        high = check.astype(BF16).astype(F32)
        pair = jnp.concatenate([high, check - high], 0).astype(BF16)
        here = parents * LANES
        lane = iota((2 * own, here), 1)
        box = lane % LANES // per_box * parents + lane // LANES
        hit = (iota((2 * own, here), 0) % own == box).astype(F32).astype(BF16)
        dens[...] = dot(pair, hit, TN)
        out_ref[...] = total[up_rows + own_rows :]
        for p in range(parents):
            target = rows3(offsets_ref, lanes_of(p, me))
            lanes = slice(p * LANES, (p + 1) * LANES)
            force = [jnp.zeros((8, LANES), F32) for _ in range(3)]
            for row in range(0, count, 8):
                d = [
                    target[c] - shell_ref[c * count + row : c * count + row + 8, :]
                    for c in range(3)
                ]
                q = [dens[c * count + row : c * count + row + 8, lanes] for c in range(3)]
                part = stokeslet(d, q)
                force = [force[c] + part[c] for c in range(3)]
            for c in range(3):
                row = p * 4 + c
                out_ref[row : row + 1, :] += jnp.sum(force[c], 0, keepdims=True)

    forces = call(
        down_body,
        shape((parents * 4, LANES), F32),
        20_000_000,
        [pltpu.VMEM((3 * count, parents * LANES), F32)],
        [VMEM] * (4 + lvls),
    )(child_ops, check_map, offsets, shell, *mids)
    forces = exchanged([forces] * lvls)

    def join_body(*refs):
        *parts, out_ref = refs
        me = lax.axis_index("lvl")
        for k, ref in enumerate(parts):
            peer = jnp.bitwise_xor(me, k)
            for p in range(parents):
                out_ref[:, lanes_of(p, peer)] = ref[p * 4 : p * 4 + 3, :]

    return call(join_body, shape((3, tall), F32), 100_000, (), [VMEM] * lvls)(*forces)


def solution(mesh):
    placed = (
        P(None, "leaf"),
        P(None, "leaf"),
        P("lvl", None, None),
        P("lvl", None, None),
        P(),
        P("lvl", "leaf", None, None),
        P("lvl", "leaf", None),
        P("lvl", None, None, None),
        P("lvl", None, None),
        P("leaf", "lvl"),
        P("leaf", "lvl"),
    )
    return jax.shard_map(
        local, mesh=mesh, in_specs=placed, out_specs=P(None, "leaf"), check_vma=False
    )
```

```python
import jax
import jax.numpy as jnp
import numpy as np
from jax import lax
from jax.experimental import pallas as pl
from jax.experimental.pallas import tpu as pltpu
from jax.sharding import PartitionSpec as P

SIDE = 6
EPSILON2 = 0.01
RADIUS = 0.525
LANES = 128
F32 = jnp.float32
BF16 = jnp.bfloat16
VMEM = pl.BlockSpec(memory_space=pltpu.VMEM)
HBM = pl.BlockSpec(memory_space=pltpu.HBM)
NN = (((1,), (0,)), ((), ()))
NT = (((1,), (1,)), ((), ()))
TN = (((0,), (0,)), ((), ()))


def surface_points(edge_count):
    levels = np.linspace(-1.0, 1.0, edge_count)
    lattice = np.stack(np.meshgrid(levels, levels, levels, indexing="ij"), 0).reshape(3, -1)
    on_shell = np.max(np.abs(lattice), 0) > 1.0 - 1e-09
    return np.asarray(lattice[:, on_shell] * RADIUS, np.float32)


def dot(a, b, dims=NN):
    return lax.dot_general(a, b, dims, preferred_element_type=F32)


def iota(shape, axis):
    return lax.broadcasted_iota(jnp.int32, shape, axis)


def factors(d):
    r2 = d[0] * d[0] + d[1] * d[1] + (d[2] * d[2] + EPSILON2)
    rs = lax.rsqrt(r2)
    weight = rs * (rs * rs)
    return rs + EPSILON2 * weight, weight


def stokeslet(d, v):
    scale, weight = factors(d)
    along = weight * (d[0] * v[0] + d[1] * v[1] + d[2] * v[2])
    return [scale * v[c] + along * d[c] for c in range(3)]


def call(body, outs, cost, scratch=(), ins=None, vmem=24, spec=VMEM):
    return pl.pallas_call(
        body,
        out_shape=outs,
        in_specs=ins,
        out_specs=spec if isinstance(spec, tuple) else jax.tree.map(lambda _: spec, outs),
        scratch_shapes=list(scratch),
        cost_estimate=pl.CostEstimate(flops=cost, bytes_accessed=1 << 20, transcendentals=0),
        compiler_params=pltpu.CompilerParams(vmem_limit_bytes=vmem << 20),
    )


def in_hbm(*arrays):
    return [pltpu.with_memory_space_constraint(array, pltpu.HBM) for array in arrays]


def start_all(sources, targets, sems):
    copies = [
        pltpu.make_async_copy(source, target, sems.at[i])
        for i, (source, target) in enumerate(zip(sources, targets))
    ]
    for copy in copies:
        copy.start()
    return copies


def held(*arrays):
    return [pltpu.VMEM(array.shape, array.dtype) for array in arrays]


def shape(dims, dtype):
    return jax.ShapeDtypeStruct(tuple(dims), dtype)


def surface_block(points, vectors, shell_ref, fields, column):
    count = shell_ref.shape[0] // 3
    for row in range(0, count, 8):
        spots = [slice(c * count + row, c * count + row + 8) for c in range(3)]
        d = [shell_ref[spots[c], :] - points[c] for c in range(3)]
        for c, value in enumerate(stokeslet(d, vectors)):
            fields[spots[c], column] = value


def blocks128(matrix):
    width = matrix.shape[1]
    fill = -width % LANES
    if fill:
        matrix = jnp.concatenate([matrix, jnp.zeros((matrix.shape[0], fill), matrix.dtype)], 1)
    return [matrix[:, k : k + LANES] for k in range(0, width, LANES)]


def local(
    offsets,
    vel_cot,
    m2l_ops,
    child_ops,
    check_map,
    leaf_dest,
    leaf_slot,
    coarse_dest,
    coarse_slot,
    near_box,
    near_dir,
):
    shell_np = surface_points(SIDE)
    count = shell_np.shape[1]
    width = m2l_ops.shape[1]
    classes = m2l_ops.shape[0]
    octants = child_ops.shape[0]
    boxes, slots = near_box.shape
    per_box = offsets.shape[1] // boxes
    parents = boxes // 8
    own = parents * octants
    leaves = lax.axis_size("leaf")
    lvls = lax.axis_size("lvl")
    pieces = -(-width // LANES)
    group = octants * per_box
    groups = parents * lvls
    assert group == LANES and own == 8 and parents == 4 and lvls * octants == 8
    assert octants == 2 and classes == parents and pieces == 4 and lvls % 2 == 0
    ids_lanes = boxes // 2
    assert width + 2 * ids_lanes <= pieces * LANES
    up_rows = pieces * parents
    leaf_rows = pieces * boxes
    own_rows = pieces * own
    tall = groups * LANES
    shell = jnp.asarray(np.repeat(shell_np.reshape(-1, 1), LANES, 1))

    leaf_owner = leaf_dest.transpose(0, 2, 3, 1)[0]
    leaf_place = leaf_slot.transpose(0, 2, 1)[0]
    coarse_owner = coarse_dest.transpose(0, 2, 3, 1)[0]
    coarse_place = coarse_slot.transpose(0, 2, 1)[0]
    near_q = near_box.T
    near_d = near_dir.T

    def lanes_of(parent, lvl):
        return pl.ds(pl.multiple_of((parent * lvls + lvl) * LANES, LANES), LANES)

    def box_row(octant, box):
        return lax.rem(octant, octants) * parents + lax.div(box, 8)

    def rows3(ref, lanes):
        return [ref[c : c + 1, lanes] for c in range(3)]

    def up_body(
        offsets_hbm,
        vel_hbm,
        shell_hbm,
        owner_hbm,
        place_hbm,
        child_hbm,
        sent_ref,
        offsets_ref,
        vel_ref,
        shell_ref,
        owner_ref,
        place_ref,
        child_ref,
        fields,
        slot_ref,
        slots_ref,
        sems,
    ):
        me = lax.axis_index("lvl")
        copies = start_all(
            (offsets_hbm, vel_hbm, shell_hbm, owner_hbm, place_hbm, child_hbm),
            (offsets_ref, vel_ref, shell_ref, owner_ref, place_ref, child_ref),
            sems,
        )
        for copy in copies[:5]:
            copy.wait()
        for p in range(parents):
            lanes = lanes_of(p, me)
            surface_block(
                rows3(offsets_ref, lanes),
                rows3(vel_ref, lanes),
                shell_ref,
                fields,
                slice(p * LANES, (p + 1) * LANES),
            )
        place = place_ref[...]
        octant = lax.rem(place, 8)
        spot = lax.div(octant, octants) * own + box_row(octant, place)
        spot = spot.astype(F32).astype(BF16)
        owner = jnp.concatenate([owner_ref[c] for c in range(classes)], 0).astype(F32).astype(BF16)
        box = iota((boxes, LANES), 0)
        octant = lax.rem(box, 8)
        lane = iota((boxes, LANES), 1)
        spread = lax.div(octant, octants) * parents + lax.div(box, 8)
        ids = []
        for half in range(2):
            kept = lax.rem(octant, 2) == half
            first = kept & (lane == spread + (LANES - 2 * ids_lanes))
            second = kept & (lane == spread + (LANES - ids_lanes))
            ids.append(
                dot(owner, first.astype(F32).astype(BF16))
                + dot(spot, second.astype(F32).astype(BF16))
            )

        here = parents * LANES
        lane = iota((own + 8 * octants, here), 1)
        row = iota((own + 8 * octants, here), 0)
        second, p = (lane % LANES) // per_box, lane // LANES
        target = jnp.where(row < own, second * parents + p, own + second * 8 + p)
        pick = (row == target).astype(F32).astype(BF16)
        leaf = dot(pick, fields[...].astype(BF16), NT)
        for k, block in enumerate(blocks128(leaf[0:own])):
            for half in range(2):
                rows = block[half * parents : (half + 1) * parents]
                slot_ref[half, k * parents : (k + 1) * parents, :] = (
                    rows + ids[half] if k == pieces - 1 else rows
                )
        leaf = leaf.astype(BF16)
        slots = (devices // 2, 2, up_rows, LANES)
        parts = [slice(0, up_rows), slice(up_rows, slot_rows)]
        leaving = [
            pltpu.make_async_copy(slots_ref.at[:, part], sent_ref.at[:, part], sems.at[6 + i])
            for i, part in enumerate(parts)
        ]

        def leave(i):
            rows = slot_ref[:, parts[i], :].astype(BF16)
            slots_ref[:, parts[i], :] = jnp.broadcast_to(rows[None], slots).reshape(
                devices, up_rows, LANES
            )
            leaving[i].start()

        leave(0)
        copies[5].wait()
        total = None
        for o in range(octants):
            part = dot(leaf[own + 8 * o : own + 8 * o + 8], child_ref[o])
            total = part if total is None else total + part
        for k, block in enumerate(blocks128(total)):
            for half in range(2):
                first = up_rows + k * parents
                slot_ref[half, first : first + parents, :] = block[0:parents]
        leave(1)
        for copy in leaving:
            copy.wait()

    slot_rows = 2 * up_rows
    devices = leaves * lvls
    up_inputs = (offsets, vel_cot, shell, leaf_owner, leaf_place, child_ops)
    sent = call(
        up_body,
        pltpu.HBM((devices, slot_rows, LANES), BF16),
        20_000_000,
        held(*up_inputs)
        + [
            pltpu.VMEM((3 * count, parents * LANES), F32),
            pltpu.VMEM((2, slot_rows, LANES), F32),
            pltpu.VMEM((devices, slot_rows, LANES), BF16),
            pltpu.SemaphoreType.DMA((8,)),
        ],
        [HBM] * 6,
        40,
        HBM,
    )(*in_hbm(*up_inputs))
    got = lax.all_to_all(sent, ("leaf", "lvl"), split_axis=0, concat_axis=0, tiled=True)

    def exchanged(values):
        peers = []
        for k in range(1, lvls):
            peers.append(lax.ppermute(values[k], "lvl", [(i, i ^ k) for i in range(lvls)]))
        return [values[0]] + peers

    pair_ops = lax.ppermute(m2l_ops, "lvl", [(i, i ^ 1) for i in range(lvls)])

    def near_body(*refs):
        sources, (near_ref, sel_ref), targets = refs[:6], refs[6:8], refs[8:14]
        columns, table, sums, sems = refs[14:]
        q_ref, dir_ref, offsets_ref, vel_ref, owner_ref, place_ref = targets
        for copy in start_all(sources, targets, sems):
            copy.wait()
        mine = lax.axis_index("leaf") * parents
        coarse = leaves * parents
        pick = jnp.concatenate(
            [
                (
                    owner_ref[c] * parents + place_ref[c : c + 1, :]
                    == mine + iota((8, coarse), 0) % parents
                ).astype(F32)
                for c in range(classes)
            ],
            0,
        ).astype(BF16)
        spread = (coarse, leaves * up_rows)
        lane = iota(spread, 1)
        for k in range(pieces):
            expand = (iota(spread, 0) == lane // up_rows * parents + lane % parents) & (
                lane % up_rows // parents == k
            )
            sel_ref[k] = dot(pick, expand.astype(F32).astype(BF16)).astype(BF16)

        left = iota((8, LANES), 1) < per_box
        for j in range(groups):
            lanes = slice(j * LANES, (j + 1) * LANES)
            tile = jnp.concatenate(
                [offsets_ref[:, lanes], vel_ref[:, lanes], jnp.zeros((2, LANES), F32)], 0
            )
            columns[lanes, :] = tile.T
            turned = pltpu.roll(tile, per_box, 1)
            table[2 * j] = jnp.where(left, tile, turned)
            table[2 * j + 1] = jnp.where(left, turned, tile)
        near_ref[...] = jnp.zeros_like(near_ref)
        ones = jnp.ones((8, LANES), BF16)

        def block(j, _):
            for h in range(2):
                box = 2 * j + h
                sources = []
                for n in range(0, slots, 2):
                    codes = [dir_ref[n + i, box] for i in range(2)]
                    moves = [
                        (
                            lax.div(code, 9) - 1,
                            lax.rem(lax.div(code, 3), 3) - 1,
                            lax.rem(code, 3) - 1,
                        )
                        for code in codes
                    ]
                    tile = jnp.where(left, table[q_ref[n, box]], table[q_ref[n + 1, box]])
                    rows = [jnp.broadcast_to(tile[c : c + 1], (8, LANES)) for c in range(6)]
                    for c in range(3):
                        rows[c] = rows[c] + jnp.where(
                            left, moves[0][c].astype(F32), moves[1][c].astype(F32)
                        )
                    sources.append(rows)
                for row in range(0, per_box, 8):
                    tile = columns[pl.ds(pl.multiple_of(box * per_box + row, 8), 8), :]
                    target = [jnp.broadcast_to(tile[:, c : c + 1], (8, LANES)) for c in range(3)]
                    force = None
                    for rows in sources:
                        part = stokeslet([target[c] - rows[c] for c in range(3)], rows[3:])
                        force = part if force is None else [x + y for x, y in zip(force, part)]
                    for c in range(3):
                        sums[c, h * per_box + row : h * per_box + row + 8, :] = force[c]
            p, lvl = lax.div(j, lvls), lax.rem(j, lvls)
            for c in range(3):
                total = dot(ones, sums[c].astype(BF16), NT)
                near_ref[lvl, pl.ds(p * 4 + c, 1), :] = total[0:1]
            return 0

        lax.fori_loop(0, groups, block, 0)

    near, select = call(
        near_body,
        (
            shape((lvls, parents * 4, LANES), F32),
            shape((pieces, 8 * classes, leaves * up_rows), BF16),
        ),
        100_000_000,
        [pltpu.SMEM(near_q.shape, jnp.int32), pltpu.SMEM(near_d.shape, jnp.int32)]
        + held(offsets, vel_cot, coarse_owner, coarse_place)
        + [
            pltpu.VMEM((tall, 8), F32),
            pltpu.VMEM((boxes, 8, LANES), F32),
            pltpu.VMEM((3, LANES, LANES), F32),
            pltpu.SemaphoreType.DMA((6,)),
        ],
        [HBM] * 6,
        24,
    )(*in_hbm(near_q, near_d, offsets, vel_cot, coarse_owner, coarse_place))

    heads = classes // 2

    def hold_body(m2l_hbm, pair_ref, near_ref, m2l_ref, head_ref, tail_ref, sems):
        copies = start_all((m2l_hbm, pair_ref.at[heads:]), (m2l_ref, tail_ref), sems)
        head_ref[...] = pair_ref[:heads]
        for copy in copies:
            copy.wait()

    own_ops, head_ops, tail_ops = call(
        hold_body,
        (
            shape(m2l_ops.shape, BF16),
            shape((heads, width, width), BF16),
            pltpu.HBM((classes - heads, width, width), BF16),
        ),
        1_000_000,
        [pltpu.SemaphoreType.DMA((2,))],
        [HBM, VMEM, VMEM],
        24,
        (VMEM, VMEM, HBM),
    )(*in_hbm(m2l_ops), pair_ops, near)

    def mid_body(got_ref, sel_ref, m2l_ref, near_ref, head_ref, tail_hbm, *refs):
        *out_refs, tail_ref, leaf_sum, sem = refs
        copy = pltpu.make_async_copy(tail_hbm, tail_ref, sem)
        copy.start()
        me = lax.axis_index("lvl")
        mine = lax.axis_index("leaf").astype(F32)
        tops = got_ref[:, up_rows:, :].astype(F32).reshape(leaves, lvls, up_rows, LANES)
        tops = jnp.sum(tops, 1).astype(BF16).reshape(leaves * up_rows, LANES)
        chosen = jnp.concatenate([dot(sel_ref[k], tops) for k in range(pieces)], 1)
        high = chosen.astype(BF16).astype(F32)
        parts = jnp.where(iota(chosen.shape, 0) % 8 < parents, high, chosen - high)

        tile = (2 * classes, LANES)
        lane, row = iota(tile, 1), iota(tile, 0)
        doubled = iota((LANES, 2 * LANES), 1)
        doubled = iota((LANES, 2 * LANES), 0) == lax.div(doubled, 8) * 4 + lax.rem(doubled, 4)
        doubled = doubled.astype(F32).astype(BF16)
        other = me + 1 - 2 * lax.rem(me, 2)
        last = slice(up_rows - 8, up_rows)
        ids = []
        for first in range(0, leaves, LANES // ids_lanes):
            owner = spot = jnp.zeros(tile, F32)
            for i in range(min(LANES // ids_lanes, leaves - first)):
                at = (first + i) * lvls
                piece = jnp.where(
                    row < classes,
                    pltpu.roll(got_ref[at + me, last, :].astype(F32), 4, 0),
                    got_ref[at + other, last, :].astype(F32),
                )
                here = lax.div(lane, ids_lanes) == i
                owner = jnp.where(here, pltpu.roll(piece, (i + 2) * ids_lanes % LANES, 1), owner)
                spot = jnp.where(here, pltpu.roll(piece, (i + 1) * ids_lanes % LANES, 1), spot)
            ids.append(dot(jnp.concatenate([owner, spot], 0).astype(BF16), doubled))
        ids = jnp.concatenate(ids, 1)[:, : devices * 8]
        spots = iota((boxes, devices * 8), 0).astype(F32)
        hits = jnp.concatenate(
            [
                (
                    (ids[c : c + 1] == mine) & (ids[2 * classes + c : 2 * classes + c + 1] == spots)
                ).astype(F32)
                for c in range(2 * classes)
            ],
            0,
        )
        upper = iota(hits.shape, 1) % 8 < 4
        hits = [jnp.where(upper, hits, 0.0).astype(BF16), jnp.where(upper, 0.0, hits).astype(BF16)]
        gathered = jnp.concatenate(
            [
                dot(hits[k % 2], got_ref[:, k // 2 * 8 : k // 2 * 8 + 8, :].reshape(devices * 8, LANES))
                for k in range(pieces)
            ],
            1,
        )[:, :width]
        total = None
        for c in range(classes):
            rows = jnp.concatenate(
                [gathered[c * boxes : (c + 1) * boxes], parts[8 * c : 8 * c + 8, :width]], 0
            )
            part = dot(rows.astype(BF16), m2l_ref[c])
            total = part if total is None else total + part
        leaf = total[:boxes]
        for c in range(classes):
            if c == heads:
                copy.wait()
            rows = gathered[(classes + c) * boxes : (classes + c + 1) * boxes]
            leaf = leaf + dot(rows.astype(BF16), head_ref[c] if c < heads else tail_ref[c - heads])
        for k, block in enumerate(blocks128(leaf)):
            leaf_sum[k * boxes : (k + 1) * boxes, :] = block
        total = total[boxes:]
        total = 0.5 * (total[0:parents] + total[parents : 2 * parents])
        total_blocks = blocks128(total)
        for k, out_ref in enumerate(out_refs):
            peer = jnp.bitwise_xor(me, k)
            for i, block in enumerate(total_blocks):
                out_ref[i * parents : (i + 1) * parents, :] = block.astype(out_ref.dtype)
            for i in range(pieces):
                rows = leaf_sum[pl.ds(pl.multiple_of(i * boxes + peer * own, own), own), :]
                out_ref[up_rows + i * own : up_rows + (i + 1) * own, :] = rows.astype(out_ref.dtype)
            out_ref[up_rows + own_rows :, :] = near_ref[peer].astype(out_ref.dtype)

    pay_rows = up_rows + own_rows + parents * 4
    mids = call(
        mid_body,
        tuple(shape((pay_rows, LANES), BF16 if k else F32) for k in range(lvls)),
        20_000_000,
        held(tail_ops) + [pltpu.VMEM((leaf_rows, LANES), F32), pltpu.SemaphoreType.DMA],
        [VMEM] * 5 + [HBM],
        40,
    )(got, select, own_ops, near, head_ops, *in_hbm(tail_ops))
    mids = exchanged(mids)

    geo_rows = parents * count

    def prep_body(
        offsets_hbm, shell_hbm, child_hbm, map_hbm, offsets_ref, shell_ref, child_ref, split_ref, scale_ref, weight_ref, map_ref, sems
    ):
        copies = start_all(
            (offsets_hbm, shell_hbm, map_hbm, child_hbm),
            (offsets_ref, shell_ref, map_ref, child_ref),
            sems,
        )
        me = lax.axis_index("lvl")
        for copy in copies[:2]:
            copy.wait()
        for p in range(parents):
            target = rows3(offsets_ref, lanes_of(p, me))
            for row in range(0, count, 8):
                d = [
                    target[c] - shell_ref[c * count + row : c * count + row + 8, :]
                    for c in range(3)
                ]
                rows = slice(p * count + row, p * count + row + 8)
                scale_ref[rows, :], weight_ref[rows, :] = factors(d)
        copies[2].wait()
        mapped = map_ref[...]
        high = mapped.astype(BF16)
        split_ref[0] = high
        split_ref[1] = (mapped - high.astype(F32)).astype(BF16)
        copies[3].wait()

    prep_inputs = (offsets, shell, child_ops, check_map)
    prepared = call(
        prep_body,
        (
            shape(offsets.shape, F32),
            shape(shell.shape, F32),
            shape(child_ops.shape, BF16),
            shape((2, width, width), BF16),
            shape((geo_rows, LANES), F32),
            shape((geo_rows, LANES), F32),
        ),
        2_000_000,
        held(check_map) + [pltpu.SemaphoreType.DMA((4,))],
        [HBM] * 4,
    )(*in_hbm(*prep_inputs))

    def down_body(offsets_ref, shell_ref, child_ref, split_ref, scale_ref, weight_ref, *refs):
        *mid_refs, out_ref, dens = refs
        me = lax.axis_index("lvl")
        total = mid_refs[0][...]
        for ref in mid_refs[1:]:
            total = total + ref[...].astype(F32)
        top = jnp.concatenate(
            [total[k * parents : (k + 1) * parents] for k in range(pieces)], 1
        )[:, :width].astype(BF16)
        lowered = jnp.concatenate([dot(top, child_ref[o], NT) for o in range(octants)], 0)
        leaf = jnp.concatenate(
            [total[up_rows + k * own : up_rows + (k + 1) * own] for k in range(pieces)], 1
        )[:, :width]
        mult = leaf + lowered
        high = mult.astype(BF16)
        pair = jnp.concatenate([high.astype(F32), mult - high.astype(F32)], 0).astype(BF16)
        first, second = dot(pair, split_ref[0]), dot(pair, split_ref[1])
        check = first[0:own] + first[own:] + second[0:own] + second[own:]
        high = check.astype(BF16).astype(F32)
        pair = jnp.concatenate([high, check - high], 0).astype(BF16)
        here = parents * LANES
        lane = iota((2 * own, here), 1)
        box = lane % LANES // per_box * parents + lane // LANES
        hit = (iota((2 * own, here), 0) % own == box).astype(F32).astype(BF16)
        dens[...] = dot(pair, hit, TN)
        out_ref[...] = total[up_rows + own_rows :]
        for p in range(parents):
            target = rows3(offsets_ref, lanes_of(p, me))
            lanes = slice(p * LANES, (p + 1) * LANES)
            force = [jnp.zeros((8, LANES), F32) for _ in range(3)]
            for row in range(0, count, 8):
                spots = [slice(c * count + row, c * count + row + 8) for c in range(3)]
                d = [target[c] - shell_ref[spots[c], :] for c in range(3)]
                q = [dens[spots[c], lanes] for c in range(3)]
                rows = slice(p * count + row, p * count + row + 8)
                scale = scale_ref[rows, :]
                along = weight_ref[rows, :] * (d[0] * q[0] + d[1] * q[1] + d[2] * q[2])
                force = [force[c] + (scale * q[c] + along * d[c]) for c in range(3)]
            for c in range(3):
                row = p * 4 + c
                out_ref[row : row + 1, :] += jnp.sum(force[c], 0, keepdims=True)

    forces = call(
        down_body,
        shape((parents * 4, LANES), F32),
        20_000_000,
        [pltpu.VMEM((3 * count, parents * LANES), F32)],
        [VMEM] * (6 + lvls),
    )(*prepared, *mids)
    forces = exchanged([forces] * lvls)

    def join_body(*refs):
        *parts, out_ref = refs
        me = lax.axis_index("lvl")
        for k, ref in enumerate(parts):
            peer = jnp.bitwise_xor(me, k)
            for p in range(parents):
                out_ref[:, lanes_of(p, peer)] = ref[p * 4 : p * 4 + 3, :]

    return call(join_body, shape((3, tall), F32), 100_000, (), [VMEM] * lvls)(*forces)


def solution(mesh):
    placed = (
        P(None, "leaf"),
        P(None, "leaf"),
        P("lvl", None, None),
        P("lvl", None, None),
        P(),
        P("lvl", "leaf", None, None),
        P("lvl", "leaf", None),
        P("lvl", None, None, None),
        P("lvl", None, None),
        P("leaf", "lvl"),
        P("leaf", "lvl"),
    )
    return jax.shard_map(
        local, mesh=mesh, in_specs=placed, out_specs=P(None, "leaf"), check_vma=False
    )
```

```python
import jax
import jax.numpy as jnp
import numpy as np
from jax import lax
from jax.experimental import pallas as pl
from jax.experimental.pallas import tpu as pltpu
from jax.sharding import PartitionSpec as P

SIDE = 6
EPSILON2 = 0.01
RADIUS = 0.525
LANES = 128
UNROLL = 4
F32 = jnp.float32
BF16 = jnp.bfloat16
VMEM = pl.BlockSpec(memory_space=pltpu.VMEM)
HBM = pl.BlockSpec(memory_space=pltpu.HBM)
NN = (((1,), (0,)), ((), ()))
NT = (((1,), (1,)), ((), ()))
TN = (((0,), (0,)), ((), ()))


def surface_points(edge_count):
    levels = np.linspace(-1.0, 1.0, edge_count)
    lattice = np.stack(np.meshgrid(levels, levels, levels, indexing="ij"), 0).reshape(3, -1)
    on_shell = np.max(np.abs(lattice), 0) > 1.0 - 1e-09
    return np.asarray(lattice[:, on_shell] * RADIUS, np.float32)


def dot(a, b, dims=NN):
    return lax.dot_general(a, b, dims, preferred_element_type=F32)


def iota(shape, axis):
    return lax.broadcasted_iota(jnp.int32, shape, axis)


def factors(d):
    r2 = d[0] * d[0] + d[1] * d[1] + (d[2] * d[2] + EPSILON2)
    rs = lax.rsqrt(r2)
    weight = rs * (rs * rs)
    return rs + EPSILON2 * weight, weight


def stokeslet(d, v):
    scale, weight = factors(d)
    along = weight * (d[0] * v[0] + d[1] * v[1] + d[2] * v[2])
    return [scale * v[c] + along * d[c] for c in range(3)]


def call(body, outs, cost, scratch=(), ins=None, vmem=24, spec=VMEM):
    return pl.pallas_call(
        body,
        out_shape=outs,
        in_specs=ins,
        out_specs=spec if isinstance(spec, tuple) else jax.tree.map(lambda _: spec, outs),
        scratch_shapes=list(scratch),
        cost_estimate=pl.CostEstimate(flops=cost, bytes_accessed=1 << 20, transcendentals=0),
        compiler_params=pltpu.CompilerParams(vmem_limit_bytes=vmem << 20),
    )


def in_hbm(*arrays):
    return [pltpu.with_memory_space_constraint(array, pltpu.HBM) for array in arrays]


def start_all(sources, targets, sems):
    copies = [
        pltpu.make_async_copy(source, target, sems.at[i])
        for i, (source, target) in enumerate(zip(sources, targets))
    ]
    for copy in copies:
        copy.start()
    return copies


def held(*arrays):
    return [pltpu.VMEM(array.shape, array.dtype) for array in arrays]


def shape(dims, dtype):
    return jax.ShapeDtypeStruct(tuple(dims), dtype)


def surface_block(points, vectors, shell_ref, fields, column):
    count = shell_ref.shape[0] // 3
    for row in range(0, count, 8):
        spots = [slice(c * count + row, c * count + row + 8) for c in range(3)]
        d = [shell_ref[spots[c], :] - points[c] for c in range(3)]
        for c, value in enumerate(stokeslet(d, vectors)):
            fields[spots[c], column] = value


def blocks128(matrix):
    width = matrix.shape[1]
    fill = -width % LANES
    if fill:
        matrix = jnp.concatenate([matrix, jnp.zeros((matrix.shape[0], fill), matrix.dtype)], 1)
    return [matrix[:, k : k + LANES] for k in range(0, width, LANES)]


def local(
    offsets,
    vel_cot,
    m2l_ops,
    child_ops,
    check_map,
    leaf_dest,
    leaf_slot,
    coarse_dest,
    coarse_slot,
    near_box,
    near_dir,
):
    shell_np = surface_points(SIDE)
    count = shell_np.shape[1]
    width = m2l_ops.shape[1]
    classes = m2l_ops.shape[0]
    octants = child_ops.shape[0]
    boxes, slots = near_box.shape
    per_box = offsets.shape[1] // boxes
    parents = boxes // 8
    own = parents * octants
    leaves = lax.axis_size("leaf")
    lvls = lax.axis_size("lvl")
    pieces = -(-width // LANES)
    group = octants * per_box
    groups = parents * lvls
    assert group == LANES and own == 8 and parents == 4 and lvls * octants == 8
    assert octants == 2 and classes == parents and pieces == 4 and lvls % 2 == 0
    ids_lanes = boxes // 2
    assert width + 2 * ids_lanes <= pieces * LANES
    up_rows = pieces * parents
    half_rows = up_rows // 2
    leaf_rows = pieces * boxes
    own_rows = pieces * own
    tall = groups * LANES
    shell = jnp.asarray(np.repeat(shell_np.reshape(-1, 1), LANES, 1))

    leaf_owner = leaf_dest.transpose(0, 2, 3, 1)[0]
    leaf_place = leaf_slot.transpose(0, 2, 1)[0]
    coarse_owner = coarse_dest.transpose(0, 2, 3, 1)[0]
    coarse_place = coarse_slot.transpose(0, 2, 1)[0]
    near_q = near_box.T
    near_d = near_dir.T

    def lanes_of(parent, lvl):
        return pl.ds(pl.multiple_of((parent * lvls + lvl) * LANES, LANES), LANES)

    def box_row(octant, box):
        return lax.rem(octant, octants) * parents + lax.div(box, 8)

    def rows3(ref, lanes):
        return [ref[c : c + 1, lanes] for c in range(3)]

    def up_body(
        offsets_hbm,
        vel_hbm,
        shell_hbm,
        owner_hbm,
        place_hbm,
        child_hbm,
        sent_ref,
        offsets_ref,
        vel_ref,
        shell_ref,
        owner_ref,
        place_ref,
        child_ref,
        fields,
        slot_ref,
        slots_ref,
        sems,
    ):
        me = lax.axis_index("lvl")
        copies = start_all(
            (offsets_hbm, vel_hbm, shell_hbm, owner_hbm, place_hbm, child_hbm),
            (offsets_ref, vel_ref, shell_ref, owner_ref, place_ref, child_ref),
            sems,
        )
        for copy in copies[:5]:
            copy.wait()
        for p in range(parents):
            lanes = lanes_of(p, me)
            surface_block(
                rows3(offsets_ref, lanes),
                rows3(vel_ref, lanes),
                shell_ref,
                fields,
                slice(p * LANES, (p + 1) * LANES),
            )
        place = place_ref[...]
        octant = lax.rem(place, 8)
        spot = lax.div(octant, octants) * own + box_row(octant, place)
        spot = spot.astype(F32).astype(BF16)
        owner = jnp.concatenate([owner_ref[c] for c in range(classes)], 0).astype(F32).astype(BF16)
        box = iota((boxes, LANES), 0)
        octant = lax.rem(box, 8)
        lane = iota((boxes, LANES), 1)
        spread = lax.div(octant, octants) * parents + lax.div(box, 8)
        ids = []
        for half in range(2):
            kept = lax.rem(octant, 2) == half
            first = kept & (lane == spread + (LANES - 2 * ids_lanes))
            second = kept & (lane == spread + (LANES - ids_lanes))
            ids.append(
                dot(owner, first.astype(F32).astype(BF16))
                + dot(spot, second.astype(F32).astype(BF16))
            )

        here = parents * LANES
        lane = iota((own + 8 * octants, here), 1)
        row = iota((own + 8 * octants, here), 0)
        second, p = (lane % LANES) // per_box, lane // LANES
        target = jnp.where(row < own, second * parents + p, own + second * 8 + p)
        pick = (row == target).astype(F32).astype(BF16)
        leaf = dot(pick, fields[...].astype(BF16), NT)
        for k, block in enumerate(blocks128(leaf[0:own])):
            for half in range(2):
                rows = block[half * parents : (half + 1) * parents]
                slot_ref[half, k * parents : (k + 1) * parents, :] = (
                    rows + ids[half] if k == pieces - 1 else rows
                )
        leaf = leaf.astype(BF16)
        parts = [slice(0, up_rows), slice(up_rows, slot_rows)]
        leaving = [
            pltpu.make_async_copy(slots_ref.at[:, part], sent_ref.at[:, part], sems.at[6 + i])
            for i, part in enumerate(parts)
        ]

        def leave(i):
            rows = slot_ref[:, parts[i], :].astype(BF16)
            high = rows.shape[1]
            slots_ref[:, parts[i], :] = jnp.broadcast_to(
                rows[None], (devices // 2, 2, high, LANES)
            ).reshape(devices, high, LANES)
            leaving[i].start()

        leave(0)
        copies[5].wait()
        total = None
        for o in range(octants):
            part = dot(leaf[own + 8 * o : own + 8 * o + 8], child_ref[o])
            total = part if total is None else total + part
        for k, block in enumerate(blocks128(total)):
            for p in range(parents):
                row = up_rows + k * (parents // 2) + p // 2
                slot_ref[p % 2, row : row + 1, :] = block[p : p + 1]
        leave(1)
        for copy in leaving:
            copy.wait()

    slot_rows = up_rows + half_rows
    devices = leaves * lvls
    up_inputs = (offsets, vel_cot, shell, leaf_owner, leaf_place, child_ops)
    sent = call(
        up_body,
        pltpu.HBM((devices, slot_rows, LANES), BF16),
        20_000_000,
        held(*up_inputs)
        + [
            pltpu.VMEM((3 * count, parents * LANES), F32),
            pltpu.VMEM((2, slot_rows, LANES), F32),
            pltpu.VMEM((devices, slot_rows, LANES), BF16),
            pltpu.SemaphoreType.DMA((8,)),
        ],
        [HBM] * 6,
        40,
        HBM,
    )(*in_hbm(*up_inputs))
    got = lax.all_to_all(sent, ("leaf", "lvl"), split_axis=0, concat_axis=0, tiled=True)

    def exchanged(values):
        peers = []
        for k in range(1, lvls):
            peers.append(lax.ppermute(values[k], "lvl", [(i, i ^ k) for i in range(lvls)]))
        return [values[0]] + peers

    pair_ops, pair_owner, pair_place = [
        lax.ppermute(value, "lvl", [(i, i ^ 1) for i in range(lvls)])
        for value in (m2l_ops, coarse_owner, coarse_place)
    ]

    def near_body(*refs):
        sources, near_ref, targets = refs[:4], refs[4], refs[5:9]
        table, sums, sems = refs[9:]
        q_ref, dir_ref, offsets_ref, vel_ref = targets
        for copy in start_all(sources, targets, sems):
            copy.wait()
        left = iota((8, LANES), 1) < per_box
        for j in range(groups):
            lanes = slice(j * LANES, (j + 1) * LANES)
            tile = jnp.concatenate(
                [offsets_ref[:, lanes], vel_ref[:, lanes], jnp.zeros((2, LANES), F32)], 0
            )
            turned = pltpu.roll(tile, per_box, 1)
            table[2 * j] = jnp.where(left, tile, turned)
            table[2 * j + 1] = jnp.where(left, turned, tile)
        near_ref[...] = jnp.zeros_like(near_ref)
        ones = jnp.ones((8, LANES), BF16)

        def block(j, slot):
            columns = jnp.where(left, table[2 * j], table[2 * j + 1]).T
            for h in range(2):
                box = 2 * j + h
                sources = []
                for n in range(0, slots, 2):
                    codes = [dir_ref[n + i, box] for i in range(2)]
                    moves = [
                        (
                            lax.div(code, 9) - 1,
                            lax.rem(lax.div(code, 3), 3) - 1,
                            lax.rem(code, 3) - 1,
                        )
                        for code in codes
                    ]
                    tile = jnp.where(left, table[q_ref[n, box]], table[q_ref[n + 1, box]])
                    rows = [jnp.broadcast_to(tile[c : c + 1], (8, LANES)) for c in range(6)]
                    for c in range(3):
                        rows[c] = rows[c] + jnp.where(
                            left, moves[0][c].astype(F32), moves[1][c].astype(F32)
                        )
                    sources.append(rows)
                for row in range(0, per_box, 8):
                    tile = columns[h * per_box + row : h * per_box + row + 8]
                    target = [jnp.broadcast_to(tile[:, c : c + 1], (8, LANES)) for c in range(3)]
                    force = None
                    for rows in sources:
                        part = stokeslet([target[c] - rows[c] for c in range(3)], rows[3:])
                        force = part if force is None else [x + y for x, y in zip(force, part)]
                    for c in range(3):
                        sums[slot, c, h * per_box + row : h * per_box + row + 8, :] = force[c]
            p, lvl = lax.div(j, lvls), lax.rem(j, lvls)
            for c in range(3):
                total = dot(ones, sums[slot, c].astype(BF16), NT)
                near_ref[lvl, pl.ds(p * 4 + c, 1), :] = total[0:1]

        def step(i, _):
            for part in range(UNROLL):
                block(i * UNROLL + part, part)
            return 0

        lax.fori_loop(0, groups // UNROLL, step, 0)

    near = call(
        near_body,
        shape((lvls, parents * 4, LANES), F32),
        100_000_000,
        [pltpu.SMEM(near_q.shape, jnp.int32), pltpu.SMEM(near_d.shape, jnp.int32)]
        + held(offsets, vel_cot)
        + [
            pltpu.VMEM((boxes, 8, LANES), F32),
            pltpu.VMEM((UNROLL, 3, LANES, LANES), F32),
            pltpu.SemaphoreType.DMA((4,)),
        ],
        [HBM] * 4,
        24,
    )(*in_hbm(near_q, near_d, offsets, vel_cot))

    heads = classes // 2

    def hold_body(
        owner_hbm, place_hbm, pair_ref, near_ref, *refs
    ):
        (pair_owner_ref, pair_place_ref), (sel_ref, head_ref, tail_ref) = refs[:2], refs[2:5]
        owner_ref, place_ref, sems = refs[5:]
        copies = start_all(
            (owner_hbm, place_hbm, pair_ref.at[heads:]), (owner_ref, place_ref, tail_ref), sems
        )
        head_ref[...] = pair_ref[:heads]
        coarse = leaves * parents
        spread = (coarse, leaves * half_rows)
        lane = iota(spread, 1)
        parent = lane // half_rows * parents + lane % 2 * 2 + lax.rem(lax.axis_index("lvl"), 2)
        for copy in copies[:2]:
            copy.wait()
        mine = lax.axis_index("leaf") * parents + iota((8, coarse), 0) % parents
        pick = jnp.concatenate(
            [
                (owners[c] * parents + places[c : c + 1, :] == mine).astype(F32)
                for owners, places in ((owner_ref, place_ref), (pair_owner_ref, pair_place_ref))
                for c in range(classes)
            ],
            0,
        ).astype(BF16)
        for k in range(pieces):
            expand = (iota(spread, 0) == parent) & (lane % half_rows // 2 == k)
            sel_ref[k] = dot(pick, expand.astype(F32).astype(BF16)).astype(BF16)
        copies[2].wait()

    select, head_ops, tail_ops = call(
        hold_body,
        (
            shape((pieces, 16 * classes, leaves * half_rows), BF16),
            shape((heads, width, width), BF16),
            pltpu.HBM((classes - heads, width, width), BF16),
        ),
        1_000_000,
        held(coarse_owner, coarse_place) + [pltpu.SemaphoreType.DMA((3,))],
        [HBM] * 2 + [VMEM] * 4,
        24,
        (VMEM, VMEM, HBM),
    )(*in_hbm(coarse_owner, coarse_place), pair_ops, near, pair_owner, pair_place)

    def mid_body(got_ref, sel_ref, m2l_ref, near_ref, head_ref, tail_hbm, *refs):
        *out_refs, tail_ref, leaf_sum, sem = refs
        copy = pltpu.make_async_copy(tail_hbm, tail_ref, sem)
        copy.start()
        me = lax.axis_index("lvl")
        mine = lax.axis_index("leaf").astype(F32)
        tops = got_ref[:, up_rows:, :].astype(F32).reshape(leaves, lvls, half_rows, LANES)
        tops = jnp.sum(tops, 1).astype(BF16).reshape(leaves * half_rows, LANES)
        chosen = jnp.concatenate([dot(sel_ref[k], tops) for k in range(pieces)], 1)
        high = chosen.astype(BF16).astype(F32)
        parts = jnp.where(iota(chosen.shape, 0) % 8 < parents, high, chosen - high)

        tile = (2 * classes, LANES)
        lane, row = iota(tile, 1), iota(tile, 0)
        doubled = iota((LANES, 2 * LANES), 1)
        doubled = iota((LANES, 2 * LANES), 0) == lax.div(doubled, 8) * 4 + lax.rem(doubled, 4)
        doubled = doubled.astype(F32).astype(BF16)
        other = me + 1 - 2 * lax.rem(me, 2)
        last = slice(up_rows - 8, up_rows)
        ids = []
        for first in range(0, leaves, LANES // ids_lanes):
            owner = spot = jnp.zeros(tile, F32)
            for i in range(min(LANES // ids_lanes, leaves - first)):
                at = (first + i) * lvls
                piece = jnp.where(
                    row < classes,
                    pltpu.roll(got_ref[at + me, last, :].astype(F32), 4, 0),
                    got_ref[at + other, last, :].astype(F32),
                )
                here = lax.div(lane, ids_lanes) == i
                owner = jnp.where(here, pltpu.roll(piece, (i + 2) * ids_lanes % LANES, 1), owner)
                spot = jnp.where(here, pltpu.roll(piece, (i + 1) * ids_lanes % LANES, 1), spot)
            ids.append(dot(jnp.concatenate([owner, spot], 0).astype(BF16), doubled))
        ids = jnp.concatenate(ids, 1)[:, : devices * 8]
        spots = iota((boxes, devices * 8), 0).astype(F32)
        hits = jnp.concatenate(
            [
                (
                    (ids[c : c + 1] == mine) & (ids[2 * classes + c : 2 * classes + c + 1] == spots)
                ).astype(F32)
                for c in range(2 * classes)
            ],
            0,
        )
        upper = iota(hits.shape, 1) % 8 < 4
        hits = [jnp.where(upper, hits, 0.0).astype(BF16), jnp.where(upper, 0.0, hits).astype(BF16)]
        gathered = jnp.concatenate(
            [
                dot(hits[k % 2], got_ref[:, k // 2 * 8 : k // 2 * 8 + 8, :].reshape(devices * 8, LANES))
                for k in range(pieces)
            ],
            1,
        )[:, :width]
        total = None
        for c in range(2 * classes):
            rows = jnp.concatenate(
                [gathered[c * boxes : (c + 1) * boxes], parts[8 * c : 8 * c + 8, :width]], 0
            )
            if c < classes:
                operator = m2l_ref[c]
            elif c < classes + heads:
                operator = head_ref[c - classes]
            else:
                if c == classes + heads:
                    copy.wait()
                operator = tail_ref[c - classes - heads]
            part = dot(rows.astype(BF16), operator)
            total = part if total is None else total + part
        leaf = total[:boxes]
        for k, block in enumerate(blocks128(leaf)):
            leaf_sum[k * boxes : (k + 1) * boxes, :] = block
        total = total[boxes:]
        total = 0.5 * (total[0:parents] + total[parents : 2 * parents])
        total_blocks = blocks128(total)
        for k, out_ref in enumerate(out_refs):
            peer = jnp.bitwise_xor(me, k)
            for i, block in enumerate(total_blocks):
                out_ref[i * parents : (i + 1) * parents, :] = block.astype(out_ref.dtype)
            for i in range(pieces):
                rows = leaf_sum[pl.ds(pl.multiple_of(i * boxes + peer * own, own), own), :]
                out_ref[up_rows + i * own : up_rows + (i + 1) * own, :] = rows.astype(out_ref.dtype)
            out_ref[up_rows + own_rows :, :] = near_ref[peer].astype(out_ref.dtype)

    pay_rows = up_rows + own_rows + parents * 4
    mids = call(
        mid_body,
        tuple(shape((pay_rows, LANES), BF16 if k else F32) for k in range(lvls)),
        20_000_000,
        held(tail_ops) + [pltpu.VMEM((leaf_rows, LANES), F32), pltpu.SemaphoreType.DMA],
        [VMEM] * 5 + [HBM],
        40,
    )(got, select, m2l_ops, near, head_ops, *in_hbm(tail_ops))
    mids = exchanged(mids)

    geo_rows = parents * count

    def prep_body(
        offsets_hbm, shell_hbm, child_hbm, map_hbm, offsets_ref, shell_ref, child_ref, split_ref, scale_ref, weight_ref, map_ref, sems
    ):
        copies = start_all(
            (offsets_hbm, shell_hbm, map_hbm, child_hbm),
            (offsets_ref, shell_ref, map_ref, child_ref),
            sems,
        )
        me = lax.axis_index("lvl")
        for copy in copies[:2]:
            copy.wait()
        for p in range(parents):
            target = rows3(offsets_ref, lanes_of(p, me))
            for row in range(0, count, 8):
                d = [
                    target[c] - shell_ref[c * count + row : c * count + row + 8, :]
                    for c in range(3)
                ]
                rows = slice(p * count + row, p * count + row + 8)
                scale_ref[rows, :], weight_ref[rows, :] = factors(d)
        copies[2].wait()
        mapped = map_ref[...]
        high = mapped.astype(BF16)
        split_ref[0] = high
        split_ref[1] = (mapped - high.astype(F32)).astype(BF16)
        copies[3].wait()

    prep_inputs = (offsets, shell, child_ops, check_map)
    prepared = call(
        prep_body,
        (
            shape(offsets.shape, F32),
            shape(shell.shape, F32),
            shape(child_ops.shape, BF16),
            shape((2, width, width), BF16),
            shape((geo_rows, LANES), F32),
            shape((geo_rows, LANES), F32),
        ),
        2_000_000,
        held(check_map) + [pltpu.SemaphoreType.DMA((4,))],
        [HBM] * 4,
    )(*in_hbm(*prep_inputs))

    def down_body(offsets_ref, shell_ref, child_ref, split_ref, scale_ref, weight_ref, *refs):
        *mid_refs, out_ref, dens = refs
        me = lax.axis_index("lvl")
        total = mid_refs[0][...]
        for ref in mid_refs[1:]:
            total = total + ref[...].astype(F32)
        top = jnp.concatenate(
            [total[k * parents : (k + 1) * parents] for k in range(pieces)], 1
        )[:, :width].astype(BF16)
        lowered = jnp.concatenate([dot(top, child_ref[o], NT) for o in range(octants)], 0)
        leaf = jnp.concatenate(
            [total[up_rows + k * own : up_rows + (k + 1) * own] for k in range(pieces)], 1
        )[:, :width]
        mult = leaf + lowered
        high = mult.astype(BF16)
        pair = jnp.concatenate([high.astype(F32), mult - high.astype(F32)], 0).astype(BF16)
        first, second = dot(pair, split_ref[0]), dot(pair, split_ref[1])
        check = first[0:own] + first[own:] + second[0:own] + second[own:]
        high = check.astype(BF16).astype(F32)
        pair = jnp.concatenate([high, check - high], 0).astype(BF16)
        here = parents * LANES
        lane = iota((2 * own, here), 1)
        box = lane % LANES // per_box * parents + lane // LANES
        hit = (iota((2 * own, here), 0) % own == box).astype(F32).astype(BF16)
        dens[...] = dot(pair, hit, TN)
        out_ref[...] = total[up_rows + own_rows :]
        for p in range(parents):
            target = rows3(offsets_ref, lanes_of(p, me))
            lanes = slice(p * LANES, (p + 1) * LANES)
            force = [jnp.zeros((8, LANES), F32) for _ in range(3)]
            for row in range(0, count, 8):
                spots = [slice(c * count + row, c * count + row + 8) for c in range(3)]
                d = [target[c] - shell_ref[spots[c], :] for c in range(3)]
                q = [dens[spots[c], lanes] for c in range(3)]
                rows = slice(p * count + row, p * count + row + 8)
                scale = scale_ref[rows, :]
                along = weight_ref[rows, :] * (d[0] * q[0] + d[1] * q[1] + d[2] * q[2])
                force = [force[c] + (scale * q[c] + along * d[c]) for c in range(3)]
            for c in range(3):
                row = p * 4 + c
                out_ref[row : row + 1, :] += jnp.sum(force[c], 0, keepdims=True)

    forces = call(
        down_body,
        shape((parents * 4, LANES), F32),
        20_000_000,
        [pltpu.VMEM((3 * count, parents * LANES), F32)],
        [VMEM] * (6 + lvls),
    )(*prepared, *mids)
    forces = exchanged([forces] * lvls)

    def join_body(*refs):
        *parts, out_ref = refs
        me = lax.axis_index("lvl")
        for k, ref in enumerate(parts):
            peer = jnp.bitwise_xor(me, k)
            for p in range(parents):
                out_ref[:, lanes_of(p, peer)] = ref[p * 4 : p * 4 + 3, :]

    return call(join_body, shape((3, tall), F32), 100_000, (), [VMEM] * lvls)(*forces)


def solution(mesh):
    placed = (
        P(None, "leaf"),
        P(None, "leaf"),
        P("lvl", None, None),
        P("lvl", None, None),
        P(),
        P("lvl", "leaf", None, None),
        P("lvl", "leaf", None),
        P("lvl", None, None, None),
        P("lvl", None, None),
        P("leaf", "lvl"),
        P("leaf", "lvl"),
    )
    return jax.shard_map(
        local, mesh=mesh, in_specs=placed, out_specs=P(None, "leaf"), check_vma=False
    )
```

```python
import jax
import jax.numpy as jnp
import numpy as np
from jax import lax
from jax.experimental import pallas as pl
from jax.experimental.pallas import tpu as pltpu
from jax.sharding import PartitionSpec as P

SIDE = 6
EPSILON2 = 0.01
RADIUS = 0.525
LANES = 128
UNROLL = 4
F32 = jnp.float32
BF16 = jnp.bfloat16
VMEM = pl.BlockSpec(memory_space=pltpu.VMEM)
HBM = pl.BlockSpec(memory_space=pltpu.HBM)
NN = (((1,), (0,)), ((), ()))
NT = (((1,), (1,)), ((), ()))
TN = (((0,), (0,)), ((), ()))


def surface_points(edge_count):
    levels = np.linspace(-1.0, 1.0, edge_count)
    lattice = np.stack(np.meshgrid(levels, levels, levels, indexing="ij"), 0).reshape(3, -1)
    on_shell = np.max(np.abs(lattice), 0) > 1.0 - 1e-09
    return np.asarray(lattice[:, on_shell] * RADIUS, np.float32)


def dot(a, b, dims=NN):
    return lax.dot_general(a, b, dims, preferred_element_type=F32)


def iota(shape, axis):
    return lax.broadcasted_iota(jnp.int32, shape, axis)


def factors(d):
    r2 = d[0] * d[0] + d[1] * d[1] + (d[2] * d[2] + EPSILON2)
    rs = lax.rsqrt(r2)
    weight = rs * (rs * rs)
    return rs + EPSILON2 * weight, weight


def scaled(d):
    r2 = d[0] * d[0] + d[1] * d[1] + (d[2] * d[2] + EPSILON2)
    rs = lax.rsqrt(r2)
    root = rs * (rs * lax.rsqrt(rs))
    return rs + EPSILON2 * (rs * (rs * rs)), [root * d[c] for c in range(3)]


def stokeslet(d, v):
    scale, weight = factors(d)
    along = weight * (d[0] * v[0] + d[1] * v[1] + d[2] * v[2])
    return [scale * v[c] + along * d[c] for c in range(3)]


def call(body, outs, cost, scratch=(), ins=None, vmem=24, spec=VMEM):
    return pl.pallas_call(
        body,
        out_shape=outs,
        in_specs=ins,
        out_specs=spec if isinstance(spec, tuple) else jax.tree.map(lambda _: spec, outs),
        scratch_shapes=list(scratch),
        cost_estimate=pl.CostEstimate(flops=cost, bytes_accessed=1 << 20, transcendentals=0),
        compiler_params=pltpu.CompilerParams(vmem_limit_bytes=vmem << 20),
    )


def in_hbm(*arrays):
    return [pltpu.with_memory_space_constraint(array, pltpu.HBM) for array in arrays]


def start_all(sources, targets, sems):
    copies = [
        pltpu.make_async_copy(source, target, sems.at[i])
        for i, (source, target) in enumerate(zip(sources, targets))
    ]
    for copy in copies:
        copy.start()
    return copies


def held(*arrays):
    return [pltpu.VMEM(array.shape, array.dtype) for array in arrays]


def shape(dims, dtype):
    return jax.ShapeDtypeStruct(tuple(dims), dtype)


def surface_block(points, vectors, shell_ref, fields, column):
    count = shell_ref.shape[0] // 3
    for row in range(0, count, 8):
        spots = [slice(c * count + row, c * count + row + 8) for c in range(3)]
        d = [shell_ref[spots[c], :] - points[c] for c in range(3)]
        for c, value in enumerate(stokeslet(d, vectors)):
            fields[spots[c], column] = value


def blocks128(matrix):
    width = matrix.shape[1]
    fill = -width % LANES
    if fill:
        matrix = jnp.concatenate([matrix, jnp.zeros((matrix.shape[0], fill), matrix.dtype)], 1)
    return [matrix[:, k : k + LANES] for k in range(0, width, LANES)]


def local(
    offsets,
    vel_cot,
    m2l_ops,
    child_ops,
    check_map,
    leaf_dest,
    leaf_slot,
    coarse_dest,
    coarse_slot,
    near_box,
    near_dir,
):
    shell_np = surface_points(SIDE)
    count = shell_np.shape[1]
    width = m2l_ops.shape[1]
    classes = m2l_ops.shape[0]
    octants = child_ops.shape[0]
    boxes, slots = near_box.shape
    per_box = offsets.shape[1] // boxes
    parents = boxes // 8
    own = parents * octants
    leaves = lax.axis_size("leaf")
    lvls = lax.axis_size("lvl")
    pieces = -(-width // LANES)
    group = octants * per_box
    groups = parents * lvls
    assert group == LANES and own == 8 and parents == 4 and lvls * octants == 8
    assert octants == 2 and classes == parents and pieces == 4 and lvls % 2 == 0
    ids_lanes = boxes // 2
    assert width + 2 * ids_lanes <= pieces * LANES
    up_rows = pieces * parents
    half_rows = up_rows // 2
    leaf_rows = pieces * boxes
    own_rows = pieces * own
    tall = groups * LANES
    shell = jnp.asarray(np.repeat(shell_np.reshape(-1, 1), LANES, 1))

    leaf_owner = leaf_dest.transpose(0, 2, 3, 1)[0]
    leaf_place = leaf_slot.transpose(0, 2, 1)[0]
    coarse_owner = coarse_dest.transpose(0, 2, 3, 1)[0]
    coarse_place = coarse_slot.transpose(0, 2, 1)[0]
    near_q = near_box.T
    near_d = near_dir.T

    def lanes_of(parent, lvl):
        return pl.ds(pl.multiple_of((parent * lvls + lvl) * LANES, LANES), LANES)

    def box_row(octant, box):
        return lax.rem(octant, octants) * parents + lax.div(box, 8)

    def rows3(ref, lanes):
        return [ref[c : c + 1, lanes] for c in range(3)]

    def up_body(
        offsets_hbm,
        vel_hbm,
        shell_hbm,
        owner_hbm,
        place_hbm,
        child_hbm,
        sent_ref,
        offsets_ref,
        vel_ref,
        shell_ref,
        owner_ref,
        place_ref,
        child_ref,
        fields,
        slot_ref,
        slots_ref,
        sems,
    ):
        me = lax.axis_index("lvl")
        copies = start_all(
            (offsets_hbm, vel_hbm, shell_hbm, owner_hbm, place_hbm, child_hbm),
            (offsets_ref, vel_ref, shell_ref, owner_ref, place_ref, child_ref),
            sems,
        )
        for copy in copies[:5]:
            copy.wait()
        for p in range(parents):
            lanes = lanes_of(p, me)
            surface_block(
                rows3(offsets_ref, lanes),
                rows3(vel_ref, lanes),
                shell_ref,
                fields,
                slice(p * LANES, (p + 1) * LANES),
            )
        place = place_ref[...]
        octant = lax.rem(place, 8)
        spot = lax.div(octant, octants) * own + box_row(octant, place)
        spot = spot.astype(F32).astype(BF16)
        owner = jnp.concatenate([owner_ref[c] for c in range(classes)], 0).astype(F32).astype(BF16)
        box = iota((boxes, LANES), 0)
        octant = lax.rem(box, 8)
        lane = iota((boxes, LANES), 1)
        spread = lax.div(octant, octants) * parents + lax.div(box, 8)
        ids = []
        for half in range(2):
            kept = lax.rem(octant, 2) == half
            first = kept & (lane == spread + (LANES - 2 * ids_lanes))
            second = kept & (lane == spread + (LANES - ids_lanes))
            ids.append(
                dot(owner, first.astype(F32).astype(BF16))
                + dot(spot, second.astype(F32).astype(BF16))
            )

        here = parents * LANES
        lane = iota((own + 8 * octants, here), 1)
        row = iota((own + 8 * octants, here), 0)
        second, p = (lane % LANES) // per_box, lane // LANES
        target = jnp.where(row < own, second * parents + p, own + second * 8 + p)
        pick = (row == target).astype(F32).astype(BF16)
        leaf = dot(pick, fields[...].astype(BF16), NT)
        for k, block in enumerate(blocks128(leaf[0:own])):
            for half in range(2):
                rows = block[half * parents : (half + 1) * parents]
                slot_ref[half, k * parents : (k + 1) * parents, :] = (
                    rows + ids[half] if k == pieces - 1 else rows
                )
        leaf = leaf.astype(BF16)
        parts = [slice(0, up_rows), slice(up_rows, slot_rows)]
        leaving = [
            pltpu.make_async_copy(slots_ref.at[:, part], sent_ref.at[:, part], sems.at[6 + i])
            for i, part in enumerate(parts)
        ]

        def leave(i):
            rows = slot_ref[:, parts[i], :].astype(BF16)
            high = rows.shape[1]
            slots_ref[:, parts[i], :] = jnp.broadcast_to(
                rows[None], (devices // 2, 2, high, LANES)
            ).reshape(devices, high, LANES)
            leaving[i].start()

        leave(0)
        copies[5].wait()
        total = None
        for o in range(octants):
            part = dot(leaf[own + 8 * o : own + 8 * o + 8], child_ref[o])
            total = part if total is None else total + part
        for k, block in enumerate(blocks128(total)):
            for p in range(parents):
                row = up_rows + k * (parents // 2) + p // 2
                slot_ref[p % 2, row : row + 1, :] = block[p : p + 1]
        leave(1)
        for copy in leaving:
            copy.wait()

    slot_rows = up_rows + half_rows
    devices = leaves * lvls
    up_inputs = (offsets, vel_cot, shell, leaf_owner, leaf_place, child_ops)
    sent = call(
        up_body,
        pltpu.HBM((devices, slot_rows, LANES), BF16),
        20_000_000,
        held(*up_inputs)
        + [
            pltpu.VMEM((3 * count, parents * LANES), F32),
            pltpu.VMEM((2, slot_rows, LANES), F32),
            pltpu.VMEM((devices, slot_rows, LANES), BF16),
            pltpu.SemaphoreType.DMA((8,)),
        ],
        [HBM] * 6,
        40,
        HBM,
    )(*in_hbm(*up_inputs))
    got = lax.all_to_all(sent, ("leaf", "lvl"), split_axis=0, concat_axis=0, tiled=True)

    def exchanged(values):
        peers = []
        for k in range(1, lvls):
            peers.append(lax.ppermute(values[k], "lvl", [(i, i ^ k) for i in range(lvls)]))
        return [values[0]] + peers

    pair_ops, pair_owner, pair_place = [
        lax.ppermute(value, "lvl", [(i, i ^ 1) for i in range(lvls)])
        for value in (m2l_ops, coarse_owner, coarse_place)
    ]

    def near_body(*refs):
        sources, near_ref, targets = refs[:4], refs[4], refs[5:9]
        table, sums, sems = refs[9:]
        q_ref, dir_ref, offsets_ref, vel_ref = targets
        for copy in start_all(sources, targets, sems):
            copy.wait()
        left = iota((8, LANES), 1) < per_box
        for j in range(groups):
            lanes = slice(j * LANES, (j + 1) * LANES)
            tile = jnp.concatenate(
                [offsets_ref[:, lanes], vel_ref[:, lanes], jnp.zeros((2, LANES), F32)], 0
            )
            turned = pltpu.roll(tile, per_box, 1)
            table[2 * j] = jnp.where(left, tile, turned)
            table[2 * j + 1] = jnp.where(left, turned, tile)
        near_ref[...] = jnp.zeros_like(near_ref)
        ones = jnp.ones((8, LANES), BF16)

        def block(j, slot):
            columns = jnp.where(left, table[2 * j], table[2 * j + 1]).T
            for h in range(2):
                box = 2 * j + h
                sources = []
                for n in range(0, slots, 2):
                    codes = [dir_ref[n + i, box] for i in range(2)]
                    moves = [
                        (
                            lax.div(code, 9) - 1,
                            lax.rem(lax.div(code, 3), 3) - 1,
                            lax.rem(code, 3) - 1,
                        )
                        for code in codes
                    ]
                    tile = jnp.where(left, table[q_ref[n, box]], table[q_ref[n + 1, box]])
                    rows = [jnp.broadcast_to(tile[c : c + 1], (8, LANES)) for c in range(6)]
                    for c in range(3):
                        rows[c] = rows[c] + jnp.where(
                            left, moves[0][c].astype(F32), moves[1][c].astype(F32)
                        )
                    sources.append(rows)
                for row in range(0, per_box, 8):
                    tile = columns[h * per_box + row : h * per_box + row + 8]
                    target = [jnp.broadcast_to(tile[:, c : c + 1], (8, LANES)) for c in range(3)]
                    force = None
                    for rows in sources:
                        part = stokeslet([target[c] - rows[c] for c in range(3)], rows[3:])
                        force = part if force is None else [x + y for x, y in zip(force, part)]
                    for c in range(3):
                        sums[slot, c, h * per_box + row : h * per_box + row + 8, :] = force[c]
            p, lvl = lax.div(j, lvls), lax.rem(j, lvls)
            for c in range(3):
                total = dot(ones, sums[slot, c].astype(BF16), NT)
                near_ref[lvl, pl.ds(p * 4 + c, 1), :] = total[0:1]

        def step(i, _):
            for part in range(UNROLL):
                block(i * UNROLL + part, part)
            return 0

        lax.fori_loop(0, groups // UNROLL, step, 0)

    near = call(
        near_body,
        shape((lvls, parents * 4, LANES), F32),
        100_000_000,
        [pltpu.SMEM(near_q.shape, jnp.int32), pltpu.SMEM(near_d.shape, jnp.int32)]
        + held(offsets, vel_cot)
        + [
            pltpu.VMEM((boxes, 8, LANES), F32),
            pltpu.VMEM((UNROLL, 3, LANES, LANES), F32),
            pltpu.SemaphoreType.DMA((4,)),
        ],
        [HBM] * 4,
        24,
    )(*in_hbm(near_q, near_d, offsets, vel_cot))

    heads = classes - 1

    def hold_body(
        owner_hbm, place_hbm, pair_ref, near_ref, *refs
    ):
        (pair_owner_ref, pair_place_ref), (sel_ref, head_ref, tail_ref) = refs[:2], refs[2:5]
        owner_ref, place_ref, sems = refs[5:]
        copies = start_all(
            (owner_hbm, place_hbm, pair_ref.at[heads:]), (owner_ref, place_ref, tail_ref), sems
        )
        head_ref[...] = pair_ref[:heads]
        coarse = leaves * parents
        spread = (coarse, leaves * half_rows)
        lane = iota(spread, 1)
        parent = lane // half_rows * parents + lane % 2 * 2 + lax.rem(lax.axis_index("lvl"), 2)
        for copy in copies[:2]:
            copy.wait()
        mine = lax.axis_index("leaf") * parents + iota((8, coarse), 0) % parents
        pick = jnp.concatenate(
            [
                (owners[c] * parents + places[c : c + 1, :] == mine).astype(F32)
                for owners, places in ((owner_ref, place_ref), (pair_owner_ref, pair_place_ref))
                for c in range(classes)
            ],
            0,
        ).astype(BF16)
        expand = (iota(spread, 0) == parent).astype(F32).astype(BF16)
        sel_ref[...] = dot(pick, expand).astype(BF16)
        copies[2].wait()

    select, head_ops, tail_ops = call(
        hold_body,
        (
            shape((16 * classes, leaves * half_rows), BF16),
            shape((heads, width, width), BF16),
            pltpu.HBM((classes - heads, width, width), BF16),
        ),
        1_000_000,
        held(coarse_owner, coarse_place) + [pltpu.SemaphoreType.DMA((3,))],
        [HBM] * 2 + [VMEM] * 4,
        24,
        (VMEM, VMEM, HBM),
    )(*in_hbm(coarse_owner, coarse_place), pair_ops, near, pair_owner, pair_place)

    def mid_body(got_ref, sel_ref, m2l_ref, near_ref, head_ref, tail_hbm, *refs):
        *out_refs, tail_ref, leaf_sum, sem = refs
        copy = pltpu.make_async_copy(tail_hbm, tail_ref, sem)
        copy.start()
        me = lax.axis_index("lvl")
        mine = lax.axis_index("leaf").astype(F32)
        tops = got_ref[:, up_rows:, :].astype(F32).reshape(leaves, lvls, half_rows, LANES)
        tops = jnp.sum(tops, 1).astype(BF16).reshape(leaves * half_rows, LANES)
        select = sel_ref[...].astype(F32)
        piece = iota(select.shape, 1) % half_rows // 2
        chosen = jnp.concatenate(
            [
                dot(jnp.where(piece == k, select, 0.0).astype(BF16), tops)
                for k in range(pieces)
            ],
            1,
        )
        high = chosen.astype(BF16).astype(F32)
        parts = jnp.where(iota(chosen.shape, 0) % 8 < parents, high, chosen - high)

        tile = (2 * classes, LANES)
        lane, row = iota(tile, 1), iota(tile, 0)
        doubled = iota((LANES, 2 * LANES), 1)
        doubled = iota((LANES, 2 * LANES), 0) == lax.div(doubled, 8) * 4 + lax.rem(doubled, 4)
        doubled = doubled.astype(F32).astype(BF16)
        other = me + 1 - 2 * lax.rem(me, 2)
        last = slice(up_rows - 8, up_rows)
        ids = []
        for first in range(0, leaves, LANES // ids_lanes):
            owner = spot = jnp.zeros(tile, F32)
            for i in range(min(LANES // ids_lanes, leaves - first)):
                at = (first + i) * lvls
                piece = jnp.where(
                    row < classes,
                    pltpu.roll(got_ref[at + me, last, :].astype(F32), 4, 0),
                    got_ref[at + other, last, :].astype(F32),
                )
                here = lax.div(lane, ids_lanes) == i
                owner = jnp.where(here, pltpu.roll(piece, (i + 2) * ids_lanes % LANES, 1), owner)
                spot = jnp.where(here, pltpu.roll(piece, (i + 1) * ids_lanes % LANES, 1), spot)
            ids.append(dot(jnp.concatenate([owner, spot], 0).astype(BF16), doubled))
        ids = jnp.concatenate(ids, 1)[:, : devices * 8]
        spots = iota((boxes, devices * 8), 0).astype(F32)
        hits = jnp.concatenate(
            [
                (
                    (ids[c : c + 1] == mine) & (ids[2 * classes + c : 2 * classes + c + 1] == spots)
                ).astype(F32)
                for c in range(2 * classes)
            ],
            0,
        )
        upper = iota(hits.shape, 1) % 8 < 4
        hits = [jnp.where(upper, hits, 0.0).astype(BF16), jnp.where(upper, 0.0, hits).astype(BF16)]
        gathered = jnp.concatenate(
            [
                dot(hits[k % 2], got_ref[:, k // 2 * 8 : k // 2 * 8 + 8, :].reshape(devices * 8, LANES))
                for k in range(pieces)
            ],
            1,
        )[:, :width]
        total = None
        for c in range(2 * classes):
            rows = jnp.concatenate(
                [gathered[c * boxes : (c + 1) * boxes], parts[8 * c : 8 * c + 8, :width]], 0
            )
            if c < classes:
                operator = m2l_ref[c]
            elif c < classes + heads:
                operator = head_ref[c - classes]
            else:
                if c == classes + heads:
                    copy.wait()
                operator = tail_ref[c - classes - heads]
            part = dot(rows.astype(BF16), operator)
            total = part if total is None else total + part
        leaf = total[:boxes]
        for k, block in enumerate(blocks128(leaf)):
            leaf_sum[k * boxes : (k + 1) * boxes, :] = block
        total = total[boxes:]
        total = 0.5 * (total[0:parents] + total[parents : 2 * parents])
        total_blocks = blocks128(total)
        for k, out_ref in enumerate(out_refs):
            peer = jnp.bitwise_xor(me, k)
            for i, block in enumerate(total_blocks):
                out_ref[i * parents : (i + 1) * parents, :] = block.astype(out_ref.dtype)
            for i in range(pieces):
                rows = leaf_sum[pl.ds(pl.multiple_of(i * boxes + peer * own, own), own), :]
                out_ref[up_rows + i * own : up_rows + (i + 1) * own, :] = rows.astype(out_ref.dtype)
            out_ref[up_rows + own_rows :, :] = near_ref[peer].astype(out_ref.dtype)

    pay_rows = up_rows + own_rows + parents * 4
    mids = call(
        mid_body,
        tuple(shape((pay_rows, LANES), BF16 if k else F32) for k in range(lvls)),
        20_000_000,
        held(tail_ops) + [pltpu.VMEM((leaf_rows, LANES), F32), pltpu.SemaphoreType.DMA],
        [VMEM] * 5 + [HBM],
        40,
    )(got, select, m2l_ops, near, head_ops, *in_hbm(tail_ops))
    mids = exchanged(mids)

    geo_rows = parents * count

    def prep_body(
        offsets_hbm, shell_hbm, child_hbm, map_hbm, child_ref, split_ref, scale_ref, turned_ref, offsets_ref, shell_ref, map_ref, sems
    ):
        copies = start_all(
            (offsets_hbm, shell_hbm, map_hbm, child_hbm),
            (offsets_ref, shell_ref, map_ref, child_ref),
            sems,
        )
        me = lax.axis_index("lvl")
        for copy in copies[:2]:
            copy.wait()
        for p in range(parents):
            target = rows3(offsets_ref, lanes_of(p, me))
            for row in range(0, count, 8):
                d = [
                    target[c] - shell_ref[c * count + row : c * count + row + 8, :]
                    for c in range(3)
                ]
                rows = slice(p * count + row, p * count + row + 8)
                scale_ref[rows, :], turned = scaled(d)
                for c in range(3):
                    turned_ref[c, rows, :] = turned[c]
        copies[2].wait()
        mapped = map_ref[...]
        high = mapped.astype(BF16)
        split_ref[0] = high
        split_ref[1] = (mapped - high.astype(F32)).astype(BF16)
        copies[3].wait()

    prep_inputs = (offsets, shell, child_ops, check_map)
    prepared = call(
        prep_body,
        (
            shape(child_ops.shape, BF16),
            shape((2, width, width), BF16),
            shape((geo_rows, LANES), F32),
            shape((3, geo_rows, LANES), F32),
        ),
        2_000_000,
        held(offsets, shell, check_map) + [pltpu.SemaphoreType.DMA((4,))],
        [HBM] * 4,
    )(*in_hbm(*prep_inputs))

    def down_body(child_ref, split_ref, scale_ref, turned_ref, *refs):
        *mid_refs, out_ref, dens = refs
        total = mid_refs[0][...]
        for ref in mid_refs[1:]:
            total = total + ref[...].astype(F32)
        top = jnp.concatenate(
            [total[k * parents : (k + 1) * parents] for k in range(pieces)], 1
        )[:, :width].astype(BF16)
        lowered = jnp.concatenate([dot(top, child_ref[o], NT) for o in range(octants)], 0)
        leaf = jnp.concatenate(
            [total[up_rows + k * own : up_rows + (k + 1) * own] for k in range(pieces)], 1
        )[:, :width]
        mult = leaf + lowered
        high = mult.astype(BF16)
        pair = jnp.concatenate([high.astype(F32), mult - high.astype(F32)], 0).astype(BF16)
        first, second = dot(pair, split_ref[0]), dot(pair, split_ref[1])
        check = first[0:own] + first[own:] + second[0:own] + second[own:]
        high = check.astype(BF16).astype(F32)
        pair = jnp.concatenate([high, check - high], 0).astype(BF16)
        here = parents * LANES
        lane = iota((2 * own, here), 1)
        box = lane % LANES // per_box * parents + lane // LANES
        hit = (iota((2 * own, here), 0) % own == box).astype(F32).astype(BF16)
        dens[...] = dot(pair, hit, TN)
        out_ref[...] = total[up_rows + own_rows :]
        for p in range(parents):
            lanes = slice(p * LANES, (p + 1) * LANES)
            force = [jnp.zeros((8, LANES), F32) for _ in range(3)]
            for row in range(0, count, 8):
                q = [dens[c * count + row : c * count + row + 8, lanes] for c in range(3)]
                rows = slice(p * count + row, p * count + row + 8)
                scale, e = scale_ref[rows, :], [turned_ref[c, rows, :] for c in range(3)]
                along = e[0] * q[0] + e[1] * q[1] + e[2] * q[2]
                force = [force[c] + (scale * q[c] + along * e[c]) for c in range(3)]
            for c in range(3):
                row = p * 4 + c
                out_ref[row : row + 1, :] += jnp.sum(force[c], 0, keepdims=True)

    forces = call(
        down_body,
        shape((parents * 4, LANES), F32),
        20_000_000,
        [pltpu.VMEM((3 * count, parents * LANES), F32)],
        [VMEM] * (4 + lvls),
    )(*prepared, *mids)
    forces = exchanged([forces] * lvls)

    def join_body(*refs):
        *parts, out_ref = refs
        me = lax.axis_index("lvl")
        for k, ref in enumerate(parts):
            peer = jnp.bitwise_xor(me, k)
            for p in range(parents):
                out_ref[:, lanes_of(p, peer)] = ref[p * 4 : p * 4 + 3, :]

    return call(join_body, shape((3, tall), F32), 100_000, (), [VMEM] * lvls)(*forces)


def solution(mesh):
    placed = (
        P(None, "leaf"),
        P(None, "leaf"),
        P("lvl", None, None),
        P("lvl", None, None),
        P(),
        P("lvl", "leaf", None, None),
        P("lvl", "leaf", None),
        P("lvl", None, None, None),
        P("lvl", None, None),
        P("leaf", "lvl"),
        P("leaf", "lvl"),
    )
    return jax.shard_map(
        local, mesh=mesh, in_specs=placed, out_specs=P(None, "leaf"), check_vma=False
    )
```
